128 devices in a mesh: depth: 4 (over x), sx: 4 (over y_hi, core), sy: 8 (over z, y_lo).
Axes of the slice: x: 4, y: 4 (y_hi: 2, y_lo: 2; y = y_hi * 2 + y_lo), z: 4, core: 2. Of those that a mesh axis runs over, the one named last changes fastest.
Arguments:
- density: float32 [128, 256, 1024], P('sx', 'sy', 'depth'), may hold values from -6 to 6
- kernel_taps: bfloat16 [2, 33], replicated, may hold values from 0.099609375 to 0.3984375
- tf_centre: float32 [8, 4], replicated, may hold values from -2 to 2
- tf_width: float32 [8, 4], replicated, may hold values from 0.4 to 1.5
- tf_color: float32 [8, 4, 3], replicated, may hold values from 0.05 to 1
- tf_opacity: float32 [8, 4], replicated, may hold values from 0.0005 to 0.004
- brick_tf: int32 [8, 16, 8], P('sx', 'sy', 'depth'), may hold values from 0 to 7
- view_order: int32 [8, 16], P('sx', 'sy'), may hold values from 0 to 1
Outputs:
- picture: float32 [4, 4, 4, 8, 256], P(None, 'sx', 'depth', None, 'sy')
The draws below stay inside these ranges and needn't reach their ends.
Inputs may be any that keep to these rules, and one draw needn't show every extreme that they name: `view_order`: 0: the viewer of that column of bricks faces z = 0; 1: it faces z = 1023.
All inputs are finite; a program needn't handle non-finite values.
Results may differ from the reference program's by a relative error of at most 0.0003.
Values may be sent and summed in bfloat16 or wider, within the bound.
A program may use at most 64 MiB of HBM per device.

```python
import math
import jax
import jax.numpy as jnp
from jax import lax

CX = 32
CY = 32
TAPS = 33
NTF = 8
NBUMP = 4
BRICKS = 2
NX = 128
NY = 256
NZ = 1024
NBX = 8
NBY = 16
NBZ = 8
N_DEPTH = 4
N_SX = 4


def with_ends(array, rng, least, largest):
    longest = array.shape.index(max(array.shape))
    spots = []
    for shift in (0, 1):
        where = [jax.random.randint(jax.random.fold_in(rng, axis), (), 0, length) for axis, length in enumerate(array.shape)]
        where[longest] = (where[longest] + shift) % array.shape[longest]
        spots.append(tuple(where))
    return array.at[spots[0]].set(least).at[spots[1]].set(largest)


def levels(key, shape, cuts, low, high):
    level, own = 1.0, jax.random.fold_in(key, 6)
    for axis_at, blocks in cuts:
        heights = jnp.exp(jax.random.uniform(jax.random.fold_in(own, axis_at), (blocks,), jnp.float32, low / len(cuts), high / len(cuts)))
        level = level * jnp.repeat(heights, shape[axis_at] // blocks).reshape([-1 if axis == axis_at else 1 for axis in range(len(shape))])
    return level


def bell_draw(stream_key, shape, width, limit, cuts=(), held_as=jnp.bfloat16):
    drawn = jax.random.normal(stream_key, shape, jnp.float32) * width
    if len(cuts) > 0:
        drawn = levels(stream_key, shape, cuts, -0.22, 0.18) * drawn
    return jnp.clip(drawn, min=-limit, max=limit).astype(held_as)


def setup_inputs(seed: int = 0) -> dict:
    arg_keys = jax.random.split(jax.random.key(seed), 9)
    density = bell_draw(arg_keys[0], (NX, NY, NZ), 1.0, 6.0, ((0, 4), (1, 8), (2, 4)), jnp.float32)
    kernel_taps = jnp.clip(jax.random.uniform(arg_keys[1], (2, TAPS), jnp.float32, 0.099609375, 0.3984375), 0.099609375, 0.3984375).astype(jnp.bfloat16)
    tf_centre = jnp.clip(jax.random.uniform(arg_keys[2], (NTF, NBUMP), jnp.float32, -2.0, 2.0), -2.0, 2.0)
    tf_width = jnp.clip(jnp.exp(jax.random.uniform(arg_keys[3], (NTF, NBUMP), jnp.float32, math.log(0.4), math.log(1.5))), 0.4, 1.5)
    tf_color = jnp.clip(jax.random.uniform(arg_keys[4], (NTF, NBUMP, 3), jnp.float32, 0.05, 1.0), 0.05, 1.0)
    tf_opacity = jnp.clip(jnp.exp(jax.random.uniform(arg_keys[5], (NTF, NBUMP), jnp.float32, math.log(0.0005), math.log(0.004))), 0.0005, 0.004)
    brick_tf = with_ends(jax.random.randint(arg_keys[6], (NBX, NBY, NBZ), 0, NTF), jax.random.fold_in(arg_keys[6], 1), 0, NTF - 1).astype(jnp.int32)
    view_order = with_ends(jax.random.randint(arg_keys[7], (NBX, NBY), 0, 2), jax.random.fold_in(arg_keys[7], 1), 0, 1).astype(jnp.int32)
    return dict(density=density, kernel_taps=kernel_taps, tf_centre=tf_centre, tf_width=tf_width, tf_color=tf_color, tf_opacity=tf_opacity, brick_tf=brick_tf, view_order=view_order)


def expand_table(table):
    return jnp.repeat(jnp.repeat(table, CX // BRICKS, 0), CY // BRICKS, 1)


def reference(density, kernel_taps, tf_centre, tf_width, tf_color, tf_opacity, brick_tf, view_order):
    thick = NZ // NBZ
    rim_width = (TAPS - 1) // 2
    taps_wide = kernel_taps.astype(jnp.float32)
    highest = lax.Precision.HIGHEST
    reverse_map = expand_table(view_order)

    def slab_image(index):
        cells = lax.dynamic_slice_in_dim(density, index * thick, thick, 2)
        coarse = cells.astype(jnp.bfloat16)
        padded = jnp.pad(coarse, ((rim_width, rim_width), (rim_width, rim_width), (0, 0))).astype(jnp.float32)
        across = jnp.zeros((NX, NY + 2 * rim_width, thick), jnp.float32)
        for offset in range(TAPS):
            across = across + taps_wide[0, offset] * padded[offset:offset + NX]
        across = lax.optimization_barrier(across.astype(jnp.bfloat16)).astype(jnp.float32)
        occlusion = jnp.zeros((NX, NY, thick), jnp.float32)
        for offset in range(TAPS):
            occlusion = occlusion + taps_wide[1, offset] * across[:, offset:offset + NY]
        shading = jax.nn.sigmoid(-occlusion)
        chosen = lax.dynamic_slice_in_dim(brick_tf, index, 1, 2)[:, :, 0]
        onehot = (chosen[:, :, None] == jnp.arange(NTF, dtype=jnp.int32)).astype(jnp.float32)
        centre = expand_table(jnp.einsum("abt,tj->abj", onehot, tf_centre, precision=highest))
        spread = expand_table(jnp.einsum("abt,tj->abj", onehot, tf_width, precision=highest))
        opacity = expand_table(jnp.einsum("abt,tj->abj", onehot, tf_opacity, precision=highest))
        colour_table = expand_table(jnp.einsum("abt,tjc->abjc", onehot, tf_color, precision=highest))
        optical = jnp.zeros((NX, NY, thick), jnp.float32)
        emission = [jnp.zeros((NX, NY, thick), jnp.float32) for channel in range(3)]
        for bump_index in range(NBUMP):
            bump_value = jnp.exp(-jnp.square((cells - centre[:, :, bump_index, None]) / spread[:, :, bump_index, None]))
            optical = optical + opacity[:, :, bump_index, None] * bump_value
            for channel in range(3):
                emission[channel] = emission[channel] + colour_table[:, :, bump_index, channel, None] * bump_value
        running = jnp.cumsum(optical, axis=2)
        summed = running[:, :, -1:]
        preceding = jnp.where(reverse_map[:, :, None] == 1, summed - running, running - optical)
        weights = jnp.exp(-preceding) * (1.0 - jnp.exp(-optical))
        colours = [jnp.sum(weights * (shading * emission[channel]), axis=2) for channel in range(3)]
        transmit = jnp.exp(-summed[:, :, 0])
        return jnp.stack(colours + [transmit])

    images = lax.map(slab_image, jnp.arange(NBZ, dtype=jnp.int32))

    def advance(carry, part_image):
        colour = carry[:3] + carry[3:] * part_image[:3]
        return jnp.concatenate([colour, carry[3:] * part_image[3:]]), None

    start = jnp.concatenate([jnp.zeros((3, NX, NY), jnp.float32), jnp.ones((1, NX, NY), jnp.float32)])
    forward, unused = lax.scan(advance, start, images)
    backward, unused_back = lax.scan(advance, start, images, reverse=True)
    final = jnp.where(reverse_map[None] == 1, backward, forward)
    picture = jnp.concatenate([final[:3], 1.0 - final[3:]])
    return picture.reshape(4, N_SX, N_DEPTH, CX // N_DEPTH, NY)
```

```python
import functools

import jax
import jax.numpy as jnp
from jax import lax
from jax.experimental import pallas as pl
from jax.experimental.pallas import tpu as pltpu
from jax.sharding import PartitionSpec as P

MESH = pl.DeviceIdType.MESH
LOG2E = 1.4426950408889634
CHUNKS = 4
SIDE = 16
CELLS = SIDE * SIDE
LANES = 128
SEGMENTS = 8


def band_tiles(taps_row, along_x, scale):
    shifted = pltpu.roll(
        jnp.broadcast_to(taps_row, (LANES, LANES)), 0, axis=1, stride=1, stride_axis=0
    ).astype(jnp.bfloat16)

    def part(index):
        return index // SIDE if along_x else index % SIDE

    def other(index):
        return index % SIDE if along_x else index // SIDE

    row = lax.broadcasted_iota(jnp.int32, (3 * CELLS, LANES), 0)
    tap = lax.broadcasted_iota(jnp.int32, (3 * CELLS, LANES), 1)
    left = (tap == part(row % CELLS) + SIDE * (row // CELLS)).astype(jnp.float32)
    first = lax.dot_general(
        left.astype(jnp.bfloat16),
        shifted,
        (((1,), (1,)), ((), ())),
        preferred_element_type=jnp.float32,
    ).astype(jnp.bfloat16)
    target = lax.broadcasted_iota(jnp.int32, (LANES, CELLS), 0)
    column = lax.broadcasted_iota(jnp.int32, (LANES, CELLS), 1)
    right = (target == part(column)).astype(jnp.float32).astype(jnp.bfloat16)
    full = jnp.dot(first, right, preferred_element_type=jnp.float32)
    row = lax.broadcasted_iota(jnp.int32, (3 * CELLS, CELLS), 0)
    column = lax.broadcasted_iota(jnp.int32, (3 * CELLS, CELLS), 1)
    keep = other(row % CELLS) == other(column)
    return jnp.where(keep, full * scale, 0.0).astype(jnp.bfloat16)


def kernel(
    counts,
    density_hbm,
    taps_ref,
    centre_ref,
    width_ref,
    color_ref,
    opacity_ref,
    brick_ref,
    order_ref,
    out_ref,
    density,
    turned,
    coarse,
    x_halo,
    across,
    y_halo,
    weighted,
    band_x,
    band_y,
    taps_wide,
    running,
    sums,
    share,
    colours,
    clear,
    colours_in,
    clear_in,
    load_sem,
    x_send,
    x_recv,
    y_send,
    y_recv,
    t_send,
    t_recv,
    c_send,
    c_recv,
):
    n_depth, n_sx, n_sy = counts
    depth, sx, sy = lax.axis_index("depth"), lax.axis_index("sx"), lax.axis_index("sy")
    rows_z = turned.shape[1]
    steps = rows_z // SEGMENTS
    chunk = rows_z // CHUNKS
    steps_chunk = steps // CHUNKS
    has = {
        ("sx", 0): sx > 0,
        ("sx", 1): sx < n_sx - 1,
        ("sy", 0): sy > 0,
        ("sy", 1): sy < n_sy - 1,
    }
    near = {
        ("sx", 0): {"sx": jnp.maximum(sx - 1, 0)},
        ("sx", 1): {"sx": jnp.minimum(sx + 1, n_sx - 1)},
        ("sy", 0): {"sy": jnp.maximum(sy - 1, 0)},
        ("sy", 1): {"sy": jnp.minimum(sy + 1, n_sy - 1)},
    }

    loads = []
    for half in range(2):
        copy = pltpu.make_async_copy(
            density_hbm.at[pl.ds(half * SIDE, SIDE)],
            density.at[pl.ds(half * SIDE, SIDE)],
            load_sem.at[half],
        )
        copy.start()
        loads.append(copy)

    barrier = pltpu.get_barrier_semaphore()
    for key, there in has.items():

        @pl.when(there)
        def _(key=key):
            pl.semaphore_signal(barrier, inc=1, device_id=near[key], device_id_type=MESH)

    for step in range(1, n_depth):
        pl.semaphore_signal(
            barrier,
            inc=1,
            device_id={"depth": lax.rem(depth + step, n_depth)},
            device_id_type=MESH,
        )

    for axis, halo in (("sx", x_halo), ("sy", y_halo)):
        for side in range(2):

            @pl.when(jnp.logical_not(has[axis, side]))
            def _(halo=halo, side=side):
                halo[side] = jnp.zeros(halo.shape[1:], halo.dtype)

    for half in range(2):
        loads[half].wait()
        for y_half in range(2):
            tile = half * 2 + y_half
            for part in range(2):
                x_at = half * SIDE + part * (SIDE // 2)
                piece = density[x_at : x_at + SIDE // 2, y_half * SIDE : (y_half + 1) * SIDE, :]
                turned[tile * 2 + part] = piece.reshape(LANES, rows_z).T

    @pl.loop(0, steps // 2)
    def _(pair):
        for block in range(8):
            tile, part = block // 2, block % 2
            half, y_half = tile // 2, tile % 2
            both = jnp.concatenate(
                [
                    turned[block, pl.ds(pair * 2, SEGMENTS, stride=steps), :],
                    turned[block, pl.ds(pair * 2 + 1, SEGMENTS, stride=steps), :],
                ],
                axis=0,
            )
            lane = y_half * CELLS + part * LANES
            coarse[half, pl.ds(pl.multiple_of(pair * 16, 16), 16), lane : lane + LANES] = (
                both.astype(jnp.bfloat16)
            )

    waits = n_depth - 1
    for there in has.values():
        waits = waits + there.astype(jnp.int32)
    pl.semaphore_wait(barrier, waits)

    def halo_copy(axis, side, at):
        source, halo, send, recv = (
            (coarse, x_halo, x_send, x_recv)
            if axis == "sx"
            else (across, y_halo, y_send, y_recv)
        )
        rows = pl.ds(at * chunk, chunk)
        return pltpu.make_async_remote_copy(
            src_ref=source.at[side, rows],
            dst_ref=halo.at[1 - side, rows],
            send_sem=send.at[side, at],
            recv_sem=recv.at[1 - side, at],
            device_id=near[axis, side],
            device_id_type=MESH,
        )

    def halo_arrival(axis, side, at):
        halo, send, recv = (
            (x_halo, x_send, x_recv) if axis == "sx" else (y_halo, y_send, y_recv)
        )
        rows = pl.ds(at * chunk, chunk)
        return pltpu.make_async_remote_copy(
            src_ref=halo.at[side, rows],
            dst_ref=halo.at[side, rows],
            send_sem=send.at[side, at],
            recv_sem=recv.at[side, at],
            device_id=near[axis, side],
            device_id_type=MESH,
        )

    for at in range(CHUNKS):
        for side in range(2):

            @pl.when(has["sx", side])
            def _(side=side, at=at):
                halo_copy("sx", side, at).start()

    taps_wide[...] = jnp.zeros(taps_wide.shape, taps_wide.dtype)
    taps_wide[0:2, 0 : taps_ref.shape[1]] = taps_ref[...].astype(jnp.float32)
    band_x[...] = band_tiles(taps_wide[0:1, :], True, 1.0)
    band_y[...] = band_tiles(taps_wide[1:2, :], False, 0.5)

    first_brick = lax.broadcasted_iota(jnp.int32, (SEGMENTS, LANES), 0) < SEGMENTS // 2

    def table(ref, tile, *rest):
        half, y_half = tile // 2, lax.rem(tile, 2)
        return jnp.where(
            first_brick,
            ref[(brick_ref[half, y_half, 0],) + rest],
            ref[(brick_ref[half, y_half, 1],) + rest],
        )

    def reversed_tile(tile):
        return order_ref[tile // 2, lax.rem(tile, 2)] == 1

    @pl.loop(0, 4)
    def _(tile):
        sign = jnp.where(reversed_tile(tile), LOG2E, -LOG2E).astype(jnp.float32)
        centre = [table(centre_ref, tile, bump) for bump in range(4)]
        width = [table(width_ref, tile, bump) for bump in range(4)]
        narrow = [-LOG2E / (each * each) for each in width]
        thick = [table(opacity_ref, tile, bump) * sign for bump in range(4)]

        def body(step, carry):
            after = []
            for part in range(2):
                block = tile * 2 + part
                cells = turned[block, pl.ds(step, SEGMENTS, stride=steps), :]
                bumps = []
                optical = None
                for bump in range(4):
                    away = cells - centre[bump]
                    value = jnp.exp2(away * away * narrow[bump])
                    bumps.append(value)
                    term = thick[bump] * value
                    optical = term if optical is None else optical + term
                nearer = carry[part] * jnp.exp2(optical)
                weight = carry[part] - nearer
                rows = pl.ds(pl.multiple_of(step * SEGMENTS, SEGMENTS), SEGMENTS)
                for bump in range(4):
                    weighted[bump, block, rows, :] = weight * bumps[bump]
                after.append(nearer)
            return tuple(after)

        ones = jnp.ones((SEGMENTS, LANES), jnp.float32)
        ends = lax.fori_loop(0, steps, body, (ones, ones), unroll=4)
        for part in range(2):
            running[tile * 2 + part] = ends[part]

    def blur(at, source, halo, band):
        rows = slice(at * chunk, (at + 1) * chunk)
        lines = []
        for half in range(2):
            for other in range(2):
                lanes = slice(other * CELLS, (other + 1) * CELLS)
                before = halo[0, rows, lanes] if half == 0 else source[0, rows, lanes]
                behind = halo[1, rows, lanes] if half == 1 else source[1, rows, lanes]
                lines.append(
                    jnp.concatenate([before, source[half, rows, lanes], behind], axis=1)
                )
        return jnp.dot(
            jnp.concatenate(lines, axis=0), band[...], preferred_element_type=jnp.float32
        )

    for at in range(CHUNKS):
        for side in range(2):

            @pl.when(has["sx", side])
            def _(side=side, at=at):
                halo_arrival("sx", side, at).wait_recv()

        result = blur(at, coarse, x_halo, band_x).astype(jnp.bfloat16)
        for half in range(2):
            for y_half in range(2):
                place = half * 2 + y_half
                across[
                    y_half, at * chunk : (at + 1) * chunk, half * CELLS : (half + 1) * CELLS
                ] = result[place * chunk : (place + 1) * chunk]
        for side in range(2):

            @pl.when(has["sy", side])
            def _(side=side, at=at):
                halo_copy("sy", side, at).start()

    sublane = lax.broadcasted_iota(jnp.int32, (SEGMENTS, LANES), 0)
    for block in range(8):
        tile, part = block // 2, block % 2
        half, y_half = tile // 2, tile % 2
        back = order_ref[half, y_half] == 1
        end = running[block]
        through = jnp.where(back, 1.0 / end, end)
        forth, aback = through, through
        for shift in (1, 2, 4):
            forth = forth * jnp.where(sublane >= shift, pltpu.roll(forth, shift, axis=0), 1.0)
            aback = aback * jnp.where(
                sublane < SEGMENTS - shift, pltpu.roll(aback, SEGMENTS - shift, axis=0), 1.0
            )
        in_front = jnp.where(
            back,
            jnp.where(sublane < SEGMENTS - 1, pltpu.roll(aback, SEGMENTS - 1, axis=0), 1.0),
            jnp.where(sublane >= 1, pltpu.roll(forth, 1, axis=0), 1.0),
        )
        share[block] = in_front * jnp.where(back, -0.5 * through, 0.5)
        owner = half * 2 + part
        for channel in range(4):
            clear[owner, channel * 2 + y_half : channel * 2 + y_half + 1, :] = aback[0:1, :]

    def depth_copy(step, source, target, send, recv):
        peer = lax.rem(depth + step, n_depth)
        return pltpu.make_async_remote_copy(
            src_ref=source.at[peer],
            dst_ref=target.at[depth],
            send_sem=send.at[step - 1],
            recv_sem=recv.at[step - 1],
            device_id={"depth": peer},
            device_id_type=MESH,
        )

    clear_copies = [
        depth_copy(step, clear, clear_in, t_send, t_recv) for step in range(1, n_depth)
    ]
    for copy in clear_copies:
        copy.start()
    clear_in[depth] = clear[depth]

    for at in range(CHUNKS):
        for side in range(2):

            @pl.when(has["sy", side])
            def _(side=side, at=at):
                halo_arrival("sy", side, at).wait_recv()

        shade = 1.0 - jnp.tanh(blur(at, across, y_halo, band_y))
        for y_half in range(2):
            for half in range(2):
                tile = half * 2 + y_half
                place = y_half * 2 + half
                for part in range(2):
                    block = tile * 2 + part
                    for bump in range(4):
                        total = None
                        for step in range(steps_chunk):
                            row = step * SEGMENTS
                            term = (
                                weighted[
                                    bump,
                                    block,
                                    at * chunk + row : at * chunk + row + SEGMENTS,
                                    :,
                                ]
                                * shade[
                                    place * chunk + row : place * chunk + row + SEGMENTS,
                                    part * LANES : (part + 1) * LANES,
                                ]
                            )
                            total = term if total is None else total + term
                        if at == 0:
                            sums[bump, block] = total
                        else:
                            sums[bump, block] += total

    for block in range(8):
        tile, part = block // 2, block % 2
        half, y_half = tile // 2, tile % 2
        owner = half * 2 + part
        for channel in range(3):
            mixed = None
            for bump in range(4):
                term = table(color_ref, tile, bump, channel) * sums[bump, block]
                mixed = term if mixed is None else mixed + term
            row = channel * 2 + y_half
            colours[owner, row : row + 1, :] = jnp.sum(mixed * share[block], axis=0, keepdims=True)
        colours[owner, 6 + y_half : 7 + y_half, :] = jnp.zeros((1, LANES), jnp.float32)

    colour_copies = [
        depth_copy(step, colours, colours_in, c_send, c_recv) for step in range(1, n_depth)
    ]
    for copy in colour_copies:
        copy.start()
    colours_in[depth] = colours[depth]

    for copy in clear_copies:
        copy.wait()
    own_half = depth // 2
    odd = lax.rem(sublane, 2) == 1
    back_rows = (
        jnp.where(odd, order_ref[own_half, 1], order_ref[own_half, 0]) == 1
    )
    ones = jnp.ones((SEGMENTS, LANES), jnp.float32)
    forth, aback = [ones], [ones]
    for at in range(n_depth):
        forth.append(forth[-1] * clear_in[at])
        aback.append(aback[-1] * clear_in[n_depth - 1 - at])
    for copy in colour_copies:
        copy.wait()
    image = None
    for at in range(n_depth):
        in_front = jnp.where(back_rows, aback[n_depth - 1 - at], forth[at])
        term = in_front * colours_in[at]
        image = term if image is None else image + term
    out_ref[...] = jnp.where(sublane >= 6, 1.0 - forth[n_depth], image)

    for axis in ("sx", "sy"):
        for side in range(2):
            for at in range(CHUNKS):

                @pl.when(has[axis, side])
                def _(axis=axis, side=side, at=at):
                    halo_copy(axis, side, at).wait_send()


def per_device(
    counts, density, kernel_taps, tf_centre, tf_width, tf_color, tf_opacity, brick_tf, view_order
):
    rows_x, rows_y, rows_z = density.shape
    n_depth = counts[0]
    f32, bf16 = jnp.float32, jnp.bfloat16
    smem = pl.BlockSpec(memory_space=pltpu.SMEM)
    vmem = pl.BlockSpec(memory_space=pltpu.VMEM)
    picture = pl.pallas_call(
        functools.partial(kernel, counts),
        out_shape=jax.ShapeDtypeStruct((8, LANES), f32),
        in_specs=[pl.BlockSpec(memory_space=pl.ANY), vmem] + [smem] * 6,
        out_specs=vmem,
        scratch_shapes=[
            pltpu.VMEM((rows_x, rows_y, rows_z), f32),
            pltpu.VMEM((8, rows_z, LANES), f32),
            pltpu.VMEM((2, rows_z, 2 * CELLS), bf16),
            pltpu.VMEM((2, rows_z, 2 * CELLS), bf16),
            pltpu.VMEM((2, rows_z, 2 * CELLS), bf16),
            pltpu.VMEM((2, rows_z, 2 * CELLS), bf16),
            pltpu.VMEM((4, 8, rows_z, LANES), f32),
            pltpu.VMEM((3 * CELLS, CELLS), bf16),
            pltpu.VMEM((3 * CELLS, CELLS), bf16),
            pltpu.VMEM((8, LANES), f32),
            pltpu.VMEM((8, SEGMENTS, LANES), f32),
            pltpu.VMEM((4, 8, SEGMENTS, LANES), f32),
            pltpu.VMEM((8, SEGMENTS, LANES), f32),
            pltpu.VMEM((n_depth, 8, LANES), f32),
            pltpu.VMEM((n_depth, 8, LANES), f32),
            pltpu.VMEM((n_depth, 8, LANES), f32),
            pltpu.VMEM((n_depth, 8, LANES), f32),
            pltpu.SemaphoreType.DMA((2,)),
            pltpu.SemaphoreType.DMA((2, CHUNKS)),
            pltpu.SemaphoreType.DMA((2, CHUNKS)),
            pltpu.SemaphoreType.DMA((2, CHUNKS)),
            pltpu.SemaphoreType.DMA((2, CHUNKS)),
            pltpu.SemaphoreType.DMA((n_depth - 1,)),
            pltpu.SemaphoreType.DMA((n_depth - 1,)),
            pltpu.SemaphoreType.DMA((n_depth - 1,)),
            pltpu.SemaphoreType.DMA((n_depth - 1,)),
        ],
        compiler_params=pltpu.CompilerParams(collective_id=0, has_side_effects=True),
    )(density, kernel_taps, tf_centre, tf_width, tf_color, tf_opacity, brick_tf, view_order)
    picture = picture.reshape(4, 2, rows_x // n_depth, SIDE).transpose(0, 2, 1, 3)
    return picture.reshape(4, 1, 1, rows_x // n_depth, rows_y)


def solution(mesh):
    counts = tuple(mesh.shape[axis] for axis in ("depth", "sx", "sy"))
    return jax.shard_map(
        functools.partial(per_device, counts),
        mesh=mesh,
        in_specs=(
            P("sx", "sy", "depth"),
            P(),
            P(),
            P(),
            P(),
            P(),
            P("sx", "sy", "depth"),
            P("sx", "sy"),
        ),
        out_specs=P(None, "sx", "depth", None, "sy"),
        check_vma=False,
    )
```

```python
import functools

import jax
import jax.numpy as jnp
from jax import lax
from jax.experimental import pallas as pl
from jax.experimental.pallas import tpu as pltpu
from jax.sharding import PartitionSpec as P

MESH = pl.DeviceIdType.MESH
LOG2E = 1.4426950408889634
CHUNKS = 4
SIDE = 16
CELLS = SIDE * SIDE
LANES = 128
SEGMENTS = 8


def band_tiles(taps_row, along_x, scale):
    shifted = pltpu.roll(
        jnp.broadcast_to(taps_row, (LANES, LANES)), 0, axis=1, stride=1, stride_axis=0
    ).astype(jnp.bfloat16)

    def part(index):
        return index // SIDE if along_x else index % SIDE

    def other(index):
        return index % SIDE if along_x else index // SIDE

    row = lax.broadcasted_iota(jnp.int32, (3 * CELLS, LANES), 0)
    tap = lax.broadcasted_iota(jnp.int32, (3 * CELLS, LANES), 1)
    left = (tap == part(row % CELLS) + SIDE * (row // CELLS)).astype(jnp.float32)
    first = lax.dot_general(
        left.astype(jnp.bfloat16),
        shifted,
        (((1,), (1,)), ((), ())),
        preferred_element_type=jnp.float32,
    ).astype(jnp.bfloat16)
    target = lax.broadcasted_iota(jnp.int32, (LANES, CELLS), 0)
    column = lax.broadcasted_iota(jnp.int32, (LANES, CELLS), 1)
    right = (target == part(column)).astype(jnp.float32).astype(jnp.bfloat16)
    full = jnp.dot(first, right, preferred_element_type=jnp.float32)
    row = lax.broadcasted_iota(jnp.int32, (3 * CELLS, CELLS), 0)
    column = lax.broadcasted_iota(jnp.int32, (3 * CELLS, CELLS), 1)
    keep = other(row % CELLS) == other(column)
    return jnp.where(keep, full * scale, 0.0).astype(jnp.bfloat16)


def kernel(
    counts,
    density_hbm,
    taps_ref,
    centre_ref,
    width_ref,
    color_ref,
    opacity_ref,
    brick_ref,
    order_ref,
    out_ref,
    density,
    turned,
    coarse,
    x_halo,
    across,
    y_halo,
    weighted,
    band_x,
    band_y,
    taps_wide,
    running,
    sums,
    share,
    colours,
    clear,
    colours_in,
    clear_in,
    load_sem,
    x_send,
    x_recv,
    y_send,
    y_recv,
    t_send,
    t_recv,
    c_send,
    c_recv,
):
    n_depth, n_sx, n_sy = counts
    depth, sx, sy = lax.axis_index("depth"), lax.axis_index("sx"), lax.axis_index("sy")
    rows_z = turned.shape[1]
    steps = rows_z // SEGMENTS
    chunk = rows_z // CHUNKS
    steps_chunk = steps // CHUNKS
    has = {
        ("sx", 0): sx > 0,
        ("sx", 1): sx < n_sx - 1,
        ("sy", 0): sy > 0,
        ("sy", 1): sy < n_sy - 1,
    }
    near = {
        ("sx", 0): {"sx": jnp.maximum(sx - 1, 0)},
        ("sx", 1): {"sx": jnp.minimum(sx + 1, n_sx - 1)},
        ("sy", 0): {"sy": jnp.maximum(sy - 1, 0)},
        ("sy", 1): {"sy": jnp.minimum(sy + 1, n_sy - 1)},
    }

    loads = []
    for half in range(2):
        copy = pltpu.make_async_copy(
            density_hbm.at[pl.ds(half * SIDE, SIDE)],
            density.at[pl.ds(half * SIDE, SIDE)],
            load_sem.at[half],
        )
        copy.start()
        loads.append(copy)

    barrier = pltpu.get_barrier_semaphore()
    for key, there in has.items():

        @pl.when(there)
        def _(key=key):
            pl.semaphore_signal(barrier, inc=1, device_id=near[key], device_id_type=MESH)

    for step in range(1, n_depth):
        pl.semaphore_signal(
            barrier,
            inc=1,
            device_id={"depth": lax.rem(depth + step, n_depth)},
            device_id_type=MESH,
        )

    for axis, halo in (("sx", x_halo), ("sy", y_halo)):
        for side in range(2):

            @pl.when(jnp.logical_not(has[axis, side]))
            def _(halo=halo, side=side):
                halo[side] = jnp.zeros(halo.shape[1:], halo.dtype)

    for half in range(2):
        loads[half].wait()
        for y_half in range(2):
            tile = half * 2 + y_half
            for part in range(2):
                x_at = half * SIDE + part * (SIDE // 2)
                piece = density[x_at : x_at + SIDE // 2, y_half * SIDE : (y_half + 1) * SIDE, :]
                turned[tile * 2 + part] = piece.reshape(LANES, rows_z).T

    @pl.loop(0, steps // 2)
    def _(pair):
        for block in range(8):
            tile, part = block // 2, block % 2
            half, y_half = tile // 2, tile % 2
            both = jnp.concatenate(
                [
                    turned[block, pl.ds(pair * 2, SEGMENTS, stride=steps), :],
                    turned[block, pl.ds(pair * 2 + 1, SEGMENTS, stride=steps), :],
                ],
                axis=0,
            )
            lane = y_half * CELLS + part * LANES
            coarse[half, pl.ds(pl.multiple_of(pair * 16, 16), 16), lane : lane + LANES] = (
                both.astype(jnp.bfloat16)
            )

    waits = n_depth - 1
    for there in has.values():
        waits = waits + there.astype(jnp.int32)
    pl.semaphore_wait(barrier, waits)

    def halo_copy(axis, side, at):
        source, halo, send, recv = (
            (coarse, x_halo, x_send, x_recv)
            if axis == "sx"
            else (across, y_halo, y_send, y_recv)
        )
        rows = pl.ds(at * chunk, chunk)
        return pltpu.make_async_remote_copy(
            src_ref=source.at[side, rows],
            dst_ref=halo.at[1 - side, rows],
            send_sem=send.at[side, at],
            recv_sem=recv.at[1 - side, at],
            device_id=near[axis, side],
            device_id_type=MESH,
        )

    def halo_arrival(axis, side, at):
        halo, send, recv = (
            (x_halo, x_send, x_recv) if axis == "sx" else (y_halo, y_send, y_recv)
        )
        rows = pl.ds(at * chunk, chunk)
        return pltpu.make_async_remote_copy(
            src_ref=halo.at[side, rows],
            dst_ref=halo.at[side, rows],
            send_sem=send.at[side, at],
            recv_sem=recv.at[side, at],
            device_id=near[axis, side],
            device_id_type=MESH,
        )

    for at in range(CHUNKS):
        for side in range(2):

            @pl.when(has["sx", side])
            def _(side=side, at=at):
                halo_copy("sx", side, at).start()

    taps_wide[...] = jnp.zeros(taps_wide.shape, taps_wide.dtype)
    taps_wide[0:2, 0 : taps_ref.shape[1]] = taps_ref[...].astype(jnp.float32)
    band_x[...] = band_tiles(taps_wide[0:1, :], True, 1.0)
    band_y[...] = band_tiles(taps_wide[1:2, :], False, 0.5)

    first_brick = lax.broadcasted_iota(jnp.int32, (SEGMENTS, LANES), 0) < SEGMENTS // 2

    def table(ref, tile, *rest):
        half, y_half = tile // 2, lax.rem(tile, 2)
        return jnp.where(
            first_brick,
            ref[rest + (brick_ref[half, y_half, 0],)],
            ref[rest + (brick_ref[half, y_half, 1],)],
        )

    def reversed_tile(tile):
        return order_ref[tile // 2, lax.rem(tile, 2)] == 1

    @pl.loop(0, 4)
    def _(tile):
        sign = jnp.where(reversed_tile(tile), LOG2E, -LOG2E).astype(jnp.float32)
        centre = [table(centre_ref, tile, bump) for bump in range(4)]
        width = [table(width_ref, tile, bump) for bump in range(4)]
        narrow = [-LOG2E / (each * each) for each in width]
        thick = [table(opacity_ref, tile, bump) * sign for bump in range(4)]

        def body(step, carry):
            after = []
            for part in range(2):
                block = tile * 2 + part
                cells = turned[block, pl.ds(step, SEGMENTS, stride=steps), :]
                bumps = []
                optical = None
                for bump in range(4):
                    away = cells - centre[bump]
                    value = jnp.exp2(away * away * narrow[bump])
                    bumps.append(value)
                    term = thick[bump] * value
                    optical = term if optical is None else optical + term
                nearer = carry[part] * jnp.exp2(optical)
                weight = carry[part] - nearer
                rows = pl.ds(pl.multiple_of(step * SEGMENTS, SEGMENTS), SEGMENTS)
                for bump in range(4):
                    weighted[bump, block, rows, :] = weight * bumps[bump]
                after.append(nearer)
            return tuple(after)

        ones = jnp.ones((SEGMENTS, LANES), jnp.float32)
        ends = lax.fori_loop(0, steps, body, (ones, ones), unroll=4)
        for part in range(2):
            running[tile * 2 + part] = ends[part]

    def blur(at, source, halo, band):
        rows = slice(at * chunk, (at + 1) * chunk)
        lines = []
        for half in range(2):
            for other in range(2):
                lanes = slice(other * CELLS, (other + 1) * CELLS)
                before = halo[0, rows, lanes] if half == 0 else source[0, rows, lanes]
                behind = halo[1, rows, lanes] if half == 1 else source[1, rows, lanes]
                lines.append(
                    jnp.concatenate([before, source[half, rows, lanes], behind], axis=1)
                )
        return jnp.dot(
            jnp.concatenate(lines, axis=0), band[...], preferred_element_type=jnp.float32
        )

    for at in range(CHUNKS):
        for side in range(2):

            @pl.when(has["sx", side])
            def _(side=side, at=at):
                halo_arrival("sx", side, at).wait_recv()

        result = blur(at, coarse, x_halo, band_x).astype(jnp.bfloat16)
        for half in range(2):
            for y_half in range(2):
                place = half * 2 + y_half
                across[
                    y_half, at * chunk : (at + 1) * chunk, half * CELLS : (half + 1) * CELLS
                ] = result[place * chunk : (place + 1) * chunk]
        for side in range(2):

            @pl.when(has["sy", side])
            def _(side=side, at=at):
                halo_copy("sy", side, at).start()

    sublane = lax.broadcasted_iota(jnp.int32, (SEGMENTS, LANES), 0)
    for block in range(8):
        tile, part = block // 2, block % 2
        half, y_half = tile // 2, tile % 2
        back = order_ref[half, y_half] == 1
        end = running[block]
        through = jnp.where(back, 1.0 / end, end)
        forth, aback = through, through
        for shift in (1, 2, 4):
            forth = forth * jnp.where(sublane >= shift, pltpu.roll(forth, shift, axis=0), 1.0)
            aback = aback * jnp.where(
                sublane < SEGMENTS - shift, pltpu.roll(aback, SEGMENTS - shift, axis=0), 1.0
            )
        in_front = jnp.where(
            back,
            jnp.where(sublane < SEGMENTS - 1, pltpu.roll(aback, SEGMENTS - 1, axis=0), 1.0),
            jnp.where(sublane >= 1, pltpu.roll(forth, 1, axis=0), 1.0),
        )
        share[block] = in_front * jnp.where(back, -0.5 * through, 0.5)
        owner = half * 2 + part
        for channel in range(4):
            clear[owner, channel * 2 + y_half : channel * 2 + y_half + 1, :] = aback[0:1, :]

    def depth_copy(step, source, target, send, recv):
        peer = lax.rem(depth + step, n_depth)
        return pltpu.make_async_remote_copy(
            src_ref=source.at[peer],
            dst_ref=target.at[depth],
            send_sem=send.at[step - 1],
            recv_sem=recv.at[step - 1],
            device_id={"depth": peer},
            device_id_type=MESH,
        )

    clear_copies = [
        depth_copy(step, clear, clear_in, t_send, t_recv) for step in range(1, n_depth)
    ]
    for copy in clear_copies:
        copy.start()
    clear_in[depth] = clear[depth]

    for at in range(CHUNKS):
        for side in range(2):

            @pl.when(has["sy", side])
            def _(side=side, at=at):
                halo_arrival("sy", side, at).wait_recv()

        shade = 1.0 - jnp.tanh(blur(at, across, y_halo, band_y))
        for y_half in range(2):
            for half in range(2):
                tile = half * 2 + y_half
                place = y_half * 2 + half
                for part in range(2):
                    block = tile * 2 + part
                    for bump in range(4):
                        total = None
                        for step in range(steps_chunk):
                            row = step * SEGMENTS
                            term = (
                                weighted[
                                    bump,
                                    block,
                                    at * chunk + row : at * chunk + row + SEGMENTS,
                                    :,
                                ]
                                * shade[
                                    place * chunk + row : place * chunk + row + SEGMENTS,
                                    part * LANES : (part + 1) * LANES,
                                ]
                            )
                            total = term if total is None else total + term
                        if at == 0:
                            sums[bump, block] = total
                        else:
                            sums[bump, block] += total

    for block in range(8):
        tile, part = block // 2, block % 2
        half, y_half = tile // 2, tile % 2
        owner = half * 2 + part
        for channel in range(3):
            mixed = None
            for bump in range(4):
                term = table(color_ref, tile, channel, bump) * sums[bump, block]
                mixed = term if mixed is None else mixed + term
            row = channel * 2 + y_half
            colours[owner, row : row + 1, :] = jnp.sum(mixed * share[block], axis=0, keepdims=True)
        colours[owner, 6 + y_half : 7 + y_half, :] = jnp.zeros((1, LANES), jnp.float32)

    colour_copies = [
        depth_copy(step, colours, colours_in, c_send, c_recv) for step in range(1, n_depth)
    ]
    for copy in colour_copies:
        copy.start()
    colours_in[depth] = colours[depth]

    for copy in clear_copies:
        copy.wait()
    own_half = depth // 2
    odd = lax.rem(sublane, 2) == 1
    back_rows = (
        jnp.where(odd, order_ref[own_half, 1], order_ref[own_half, 0]) == 1
    )
    ones = jnp.ones((SEGMENTS, LANES), jnp.float32)
    forth, aback = [ones], [ones]
    for at in range(n_depth):
        forth.append(forth[-1] * clear_in[at])
        aback.append(aback[-1] * clear_in[n_depth - 1 - at])
    for copy in colour_copies:
        copy.wait()
    image = None
    for at in range(n_depth):
        in_front = jnp.where(back_rows, aback[n_depth - 1 - at], forth[at])
        term = in_front * colours_in[at]
        image = term if image is None else image + term
    image = jnp.where(sublane >= 6, 1.0 - forth[n_depth], image)
    low = lax.broadcasted_iota(jnp.int32, (SEGMENTS, LANES), 1) < SIDE
    for channel in range(4):
        halves = []
        for y_half in range(2):
            row = channel * 2 + y_half
            line = jnp.broadcast_to(image[row : row + 1, :], (SEGMENTS, LANES))
            for bit in (4, 2, 1):
                line = jnp.where(
                    (sublane & bit) != 0, pltpu.roll(line, LANES - SIDE * bit, axis=1), line
                )
            halves.append(pltpu.roll(line, SIDE, axis=1) if y_half else line)
        out_ref[channel] = jnp.where(low, halves[0], halves[1])[:, : 2 * SIDE]

    for axis in ("sx", "sy"):
        for side in range(2):
            for at in range(CHUNKS):

                @pl.when(has[axis, side])
                def _(axis=axis, side=side, at=at):
                    halo_copy(axis, side, at).wait_send()


def per_device(
    counts, density, kernel_taps, tf_centre, tf_width, tf_color, tf_opacity, brick_tf, view_order
):
    rows_x, rows_y, rows_z = density.shape
    n_depth = counts[0]
    f32, bf16 = jnp.float32, jnp.bfloat16
    smem = pl.BlockSpec(memory_space=pltpu.SMEM)
    vmem = pl.BlockSpec(memory_space=pltpu.VMEM)
    picture = pl.pallas_call(
        functools.partial(kernel, counts),
        out_shape=jax.ShapeDtypeStruct((4, rows_x // n_depth, rows_y), f32),
        in_specs=[pl.BlockSpec(memory_space=pl.ANY), vmem] + [smem] * 6,
        out_specs=vmem,
        scratch_shapes=[
            pltpu.VMEM((rows_x, rows_y, rows_z), f32),
            pltpu.VMEM((8, rows_z, LANES), f32),
            pltpu.VMEM((2, rows_z, 2 * CELLS), bf16),
            pltpu.VMEM((2, rows_z, 2 * CELLS), bf16),
            pltpu.VMEM((2, rows_z, 2 * CELLS), bf16),
            pltpu.VMEM((2, rows_z, 2 * CELLS), bf16),
            pltpu.VMEM((4, 8, rows_z, LANES), f32),
            pltpu.VMEM((3 * CELLS, CELLS), bf16),
            pltpu.VMEM((3 * CELLS, CELLS), bf16),
            pltpu.VMEM((8, LANES), f32),
            pltpu.VMEM((8, SEGMENTS, LANES), f32),
            pltpu.VMEM((4, 8, SEGMENTS, LANES), f32),
            pltpu.VMEM((8, SEGMENTS, LANES), f32),
            pltpu.VMEM((n_depth, 8, LANES), f32),
            pltpu.VMEM((n_depth, 8, LANES), f32),
            pltpu.VMEM((n_depth, 8, LANES), f32),
            pltpu.VMEM((n_depth, 8, LANES), f32),
            pltpu.SemaphoreType.DMA((2,)),
            pltpu.SemaphoreType.DMA((2, CHUNKS)),
            pltpu.SemaphoreType.DMA((2, CHUNKS)),
            pltpu.SemaphoreType.DMA((2, CHUNKS)),
            pltpu.SemaphoreType.DMA((2, CHUNKS)),
            pltpu.SemaphoreType.DMA((n_depth - 1,)),
            pltpu.SemaphoreType.DMA((n_depth - 1,)),
            pltpu.SemaphoreType.DMA((n_depth - 1,)),
            pltpu.SemaphoreType.DMA((n_depth - 1,)),
        ],
        compiler_params=pltpu.CompilerParams(collective_id=0, has_side_effects=True),
    )(
        density,
        kernel_taps,
        tf_centre.T,
        tf_width.T,
        tf_color.transpose(2, 1, 0),
        tf_opacity.T,
        brick_tf,
        view_order,
    )
    return picture.reshape(4, 1, 1, rows_x // n_depth, rows_y)


def solution(mesh):
    counts = tuple(mesh.shape[axis] for axis in ("depth", "sx", "sy"))
    return jax.shard_map(
        functools.partial(per_device, counts),
        mesh=mesh,
        in_specs=(
            P("sx", "sy", "depth"),
            P(),
            P(),
            P(),
            P(),
            P(),
            P("sx", "sy", "depth"),
            P("sx", "sy"),
        ),
        out_specs=P(None, "sx", "depth", None, "sy"),
        check_vma=False,
    )
```

```python
import functools

import jax
import jax.numpy as jnp
from jax import lax
from jax.experimental import pallas as pl
from jax.experimental.pallas import tpu as pltpu
from jax.sharding import PartitionSpec as P

MESH = pl.DeviceIdType.MESH
LOG2E = 1.4426950408889634
CHUNKS = 4
SIDE = 16
CELLS = SIDE * SIDE
LANES = 128
SEGMENTS = 8


def band_tiles(taps_row, along_x, scale):
    shifted = pltpu.roll(
        jnp.broadcast_to(taps_row, (LANES, LANES)), 0, axis=1, stride=1, stride_axis=0
    ).astype(jnp.bfloat16)

    def part(index):
        return index // SIDE if along_x else index % SIDE

    def other(index):
        return index % SIDE if along_x else index // SIDE

    row = lax.broadcasted_iota(jnp.int32, (3 * CELLS, LANES), 0)
    tap = lax.broadcasted_iota(jnp.int32, (3 * CELLS, LANES), 1)
    left = (tap == part(row % CELLS) + SIDE * (row // CELLS)).astype(jnp.float32)
    first = lax.dot_general(
        left.astype(jnp.bfloat16),
        shifted,
        (((1,), (1,)), ((), ())),
        preferred_element_type=jnp.float32,
    ).astype(jnp.bfloat16)
    target = lax.broadcasted_iota(jnp.int32, (LANES, CELLS), 0)
    column = lax.broadcasted_iota(jnp.int32, (LANES, CELLS), 1)
    right = (target == part(column)).astype(jnp.float32).astype(jnp.bfloat16)
    full = jnp.dot(first, right, preferred_element_type=jnp.float32)
    row = lax.broadcasted_iota(jnp.int32, (3 * CELLS, CELLS), 0)
    column = lax.broadcasted_iota(jnp.int32, (3 * CELLS, CELLS), 1)
    keep = other(row % CELLS) == other(column)
    return jnp.where(keep, full * scale, 0.0).astype(jnp.bfloat16)


def kernel(
    counts,
    density_hbm,
    taps_ref,
    centre_ref,
    width_ref,
    color_ref,
    opacity_ref,
    brick_ref,
    order_ref,
    out_ref,
    density,
    turned,
    coarse,
    x_halo,
    across,
    y_halo,
    weighted,
    band_x,
    band_y,
    taps_wide,
    running,
    sums,
    share,
    colours,
    clear,
    colours_in,
    clear_in,
    load_sem,
    x_send,
    x_recv,
    y_send,
    y_recv,
    t_send,
    t_recv,
    c_send,
    c_recv,
):
    n_depth, n_sx, n_sy = counts
    depth, sx, sy = lax.axis_index("depth"), lax.axis_index("sx"), lax.axis_index("sy")
    rows_z = turned.shape[1]
    steps = rows_z // SEGMENTS
    chunk = rows_z // CHUNKS
    steps_chunk = steps // CHUNKS
    has = {
        ("sx", 0): sx > 0,
        ("sx", 1): sx < n_sx - 1,
        ("sy", 0): sy > 0,
        ("sy", 1): sy < n_sy - 1,
    }
    near = {
        ("sx", 0): {"sx": jnp.maximum(sx - 1, 0)},
        ("sx", 1): {"sx": jnp.minimum(sx + 1, n_sx - 1)},
        ("sy", 0): {"sy": jnp.maximum(sy - 1, 0)},
        ("sy", 1): {"sy": jnp.minimum(sy + 1, n_sy - 1)},
    }

    near_half = 1 - lax.rem(sx, 2)
    far_half = lax.rem(sx, 2)
    has_far = jnp.logical_and(sx > 0, sx < n_sx - 1)
    near_core = {"sx": sx + 2 * near_half - 1}
    far_core = {"sx": jnp.clip(sx + 2 * far_half - 1, 0, n_sx - 1)}

    loads = []
    for half in range(2):
        copy = pltpu.make_async_copy(
            density_hbm.at[pl.ds(half * SIDE, SIDE)],
            density.at[pl.ds(half * SIDE, SIDE)],
            load_sem.at[half],
        )
        copy.start()
        loads.append(copy)

    barrier = pltpu.get_barrier_semaphore()
    for key, there in has.items():

        @pl.when(there)
        def _(key=key):
            pl.semaphore_signal(barrier, inc=1, device_id=near[key], device_id_type=MESH)

    for step in range(1, n_depth):
        pl.semaphore_signal(
            barrier,
            inc=1,
            device_id={"depth": lax.rem(depth + step, n_depth)},
            device_id_type=MESH,
        )

    for axis, halo in (("sx", x_halo), ("sy", y_halo)):
        for side in range(2):

            @pl.when(jnp.logical_not(has[axis, side]))
            def _(halo=halo, side=side):
                halo[side] = jnp.zeros(halo.shape[1:], halo.dtype)

    for half in range(2):
        loads[half].wait()
        for y_half in range(2):
            tile = half * 2 + y_half
            for part in range(2):
                x_at = half * SIDE + part * (SIDE // 2)
                piece = density[x_at : x_at + SIDE // 2, y_half * SIDE : (y_half + 1) * SIDE, :]
                turned[tile * 2 + part] = piece.reshape(LANES, rows_z).T

    waits = n_depth - 1
    for there in has.values():
        waits = waits + there.astype(jnp.int32)
    pl.semaphore_wait(barrier, waits)

    def x_copy(side, core, at):
        rows = pl.ds(at * chunk, chunk)
        return pltpu.make_async_remote_copy(
            src_ref=coarse.at[side, rows],
            dst_ref=x_halo.at[1 - side, rows],
            send_sem=x_send.at[side, at],
            recv_sem=x_recv.at[1 - side, at],
            device_id=core,
            device_id_type=MESH,
        )

    def x_arrival(side, core, at):
        rows = pl.ds(at * chunk, chunk)
        return pltpu.make_async_remote_copy(
            src_ref=x_halo.at[side, rows],
            dst_ref=x_halo.at[side, rows],
            send_sem=x_send.at[side, at],
            recv_sem=x_recv.at[side, at],
            device_id=core,
            device_id_type=MESH,
        )

    def y_copy(side, half, at):
        rows = pl.ds(at * chunk, chunk)
        return pltpu.make_async_remote_copy(
            src_ref=across.at[side, half, rows],
            dst_ref=y_halo.at[1 - side, half, rows],
            send_sem=y_send.at[side, half, at],
            recv_sem=y_recv.at[1 - side, half, at],
            device_id=near["sy", side],
            device_id_type=MESH,
        )

    def y_arrival(side, half, at):
        rows = pl.ds(at * chunk, chunk)
        return pltpu.make_async_remote_copy(
            src_ref=y_halo.at[side, half, rows],
            dst_ref=y_halo.at[side, half, rows],
            send_sem=y_send.at[side, half, at],
            recv_sem=y_recv.at[side, half, at],
            device_id=near["sy", side],
            device_id_type=MESH,
        )

    for at in range(CHUNKS):

        @pl.loop(at * (steps_chunk // 2), (at + 1) * (steps_chunk // 2))
        def _(pair):
            for block in range(8):
                tile, part = block // 2, block % 2
                half, y_half = tile // 2, tile % 2
                both = jnp.concatenate(
                    [
                        turned[block, pl.ds(pair * 2, SEGMENTS, stride=steps), :],
                        turned[block, pl.ds(pair * 2 + 1, SEGMENTS, stride=steps), :],
                    ],
                    axis=0,
                )
                lane = y_half * CELLS + part * LANES
                coarse[half, pl.ds(pl.multiple_of(pair * 16, 16), 16), lane : lane + LANES] = (
                    both.astype(jnp.bfloat16)
                )

        @pl.when(has_far)
        def _(at=at):
            x_copy(far_half, far_core, at).start()

        x_copy(near_half, near_core, at).start()

    taps_wide[...] = jnp.zeros(taps_wide.shape, taps_wide.dtype)
    taps_wide[0:2, 0 : taps_ref.shape[1]] = taps_ref[...].astype(jnp.float32)
    band_x[...] = band_tiles(taps_wide[0:1, :], True, 1.0)
    band_y[...] = band_tiles(taps_wide[1:2, :], False, 0.5)

    first_brick = lax.broadcasted_iota(jnp.int32, (SEGMENTS, LANES), 0) < SEGMENTS // 2

    def table(ref, tile, *rest):
        half, y_half = tile // 2, lax.rem(tile, 2)
        return jnp.where(
            first_brick,
            ref[rest + (brick_ref[half, y_half, 0],)],
            ref[rest + (brick_ref[half, y_half, 1],)],
        )

    def reversed_tile(tile):
        return order_ref[tile // 2, lax.rem(tile, 2)] == 1

    def bumps_of(tile):
        sign = jnp.where(reversed_tile(tile), LOG2E, -LOG2E).astype(jnp.float32)
        centre = [table(centre_ref, tile, bump) for bump in range(4)]
        width = [table(width_ref, tile, bump) for bump in range(4)]
        narrow = [-LOG2E / (each * each) for each in width]
        thick = [table(opacity_ref, tile, bump) * sign for bump in range(4)]

        def body(step, carry):
            after = []
            for part in range(2):
                block = tile * 2 + part
                cells = turned[block, pl.ds(step, SEGMENTS, stride=steps), :]
                bumps = []
                optical = None
                for bump in range(4):
                    away = cells - centre[bump]
                    value = jnp.exp2(away * away * narrow[bump])
                    bumps.append(value)
                    term = thick[bump] * value
                    optical = term if optical is None else optical + term
                nearer = carry[part] * jnp.exp2(optical)
                weight = carry[part] - nearer
                rows = pl.ds(pl.multiple_of(step * SEGMENTS, SEGMENTS), SEGMENTS)
                for bump in range(4):
                    weighted[bump, block, rows, :] = weight * bumps[bump]
                after.append(nearer)
            return tuple(after)

        ones = jnp.ones((SEGMENTS, LANES), jnp.float32)
        ends = lax.fori_loop(0, steps, body, (ones, ones), unroll=4)
        for part in range(2):
            running[tile * 2 + part] = ends[part]

    def blur_x(half, at):
        rows = slice(at * chunk, (at + 1) * chunk)
        inner, outer = [], []
        for y_half in range(2):
            lanes = slice(y_half * CELLS, (y_half + 1) * CELLS)
            inner.append(
                jnp.concatenate([coarse[0, rows, lanes], coarse[1, rows, lanes]], axis=1)
            )
            outer.append(x_halo[half, rows, lanes])
        inner_at = pl.multiple_of((1 - half) * CELLS, CELLS)
        outer_at = pl.multiple_of(half * (2 * CELLS), CELLS)
        result = jnp.dot(
            jnp.concatenate(inner, axis=0),
            band_x[pl.ds(inner_at, 2 * CELLS), :],
            preferred_element_type=jnp.float32,
        ) + jnp.dot(
            jnp.concatenate(outer, axis=0),
            band_x[pl.ds(outer_at, CELLS), :],
            preferred_element_type=jnp.float32,
        )
        result = result.astype(jnp.bfloat16)
        for y_half in range(2):
            across[y_half, half, rows, :] = result[y_half * chunk : (y_half + 1) * chunk]
        for side in range(2):

            @pl.when(has["sy", side])
            def _(side=side):
                y_copy(side, half, at).start()

    for at in range(CHUNKS):
        x_arrival(near_half, near_core, at).wait_recv()
        blur_x(near_half, at)

    @pl.loop(near_half * 2, near_half * 2 + 2)
    def _(tile):
        bumps_of(tile)

    for at in range(CHUNKS):

        @pl.when(has_far)
        def _(at=at):
            x_arrival(far_half, far_core, at).wait_recv()

        blur_x(far_half, at)

    @pl.loop(far_half * 2, far_half * 2 + 2)
    def _(tile):
        bumps_of(tile)

    sublane = lax.broadcasted_iota(jnp.int32, (SEGMENTS, LANES), 0)
    for block in range(8):
        tile, part = block // 2, block % 2
        half, y_half = tile // 2, tile % 2
        back = order_ref[half, y_half] == 1
        end = running[block]
        through = jnp.where(back, 1.0 / end, end)
        forth, aback = through, through
        for shift in (1, 2, 4):
            forth = forth * jnp.where(sublane >= shift, pltpu.roll(forth, shift, axis=0), 1.0)
            aback = aback * jnp.where(
                sublane < SEGMENTS - shift, pltpu.roll(aback, SEGMENTS - shift, axis=0), 1.0
            )
        in_front = jnp.where(
            back,
            jnp.where(sublane < SEGMENTS - 1, pltpu.roll(aback, SEGMENTS - 1, axis=0), 1.0),
            jnp.where(sublane >= 1, pltpu.roll(forth, 1, axis=0), 1.0),
        )
        share[block] = in_front * jnp.where(back, -0.5 * through, 0.5)
        owner = half * 2 + part
        for channel in range(4):
            clear[owner, channel * 2 + y_half : channel * 2 + y_half + 1, :] = aback[0:1, :]

    def depth_copy(step, source, target, send, recv):
        peer = lax.rem(depth + step, n_depth)
        return pltpu.make_async_remote_copy(
            src_ref=source.at[peer],
            dst_ref=target.at[depth],
            send_sem=send.at[step - 1],
            recv_sem=recv.at[step - 1],
            device_id={"depth": peer},
            device_id_type=MESH,
        )

    clear_copies = [
        depth_copy(step, clear, clear_in, t_send, t_recv) for step in range(1, n_depth)
    ]
    for copy in clear_copies:
        copy.start()
    clear_in[depth] = clear[depth]

    for half in (near_half, far_half):
        for at in range(CHUNKS):
            for side in range(2):

                @pl.when(has["sy", side])
                def _(side=side, at=at, half=half):
                    y_arrival(side, half, at).wait_recv()

            rows = slice(at * chunk, (at + 1) * chunk)
            before, first, second, behind = (
                y_halo[0, half, rows, :],
                across[0, half, rows, :],
                across[1, half, rows, :],
                y_halo[1, half, rows, :],
            )
            occlusion = jnp.dot(
                jnp.concatenate(
                    [
                        jnp.concatenate([before, first, second], axis=1),
                        jnp.concatenate([first, second, behind], axis=1),
                    ],
                    axis=0,
                ),
                band_y[...],
                preferred_element_type=jnp.float32,
            )
            shade = 1.0 - jnp.tanh(occlusion)
            for y_half in range(2):
                for part in range(2):
                    block = half * 4 + y_half * 2 + part
                    for bump in range(4):
                        total = None
                        for step in range(steps_chunk):
                            row = step * SEGMENTS
                            term = (
                                weighted[
                                    bump,
                                    block,
                                    at * chunk + row : at * chunk + row + SEGMENTS,
                                    :,
                                ]
                                * shade[
                                    y_half * chunk + row : y_half * chunk + row + SEGMENTS,
                                    part * LANES : (part + 1) * LANES,
                                ]
                            )
                            total = term if total is None else total + term
                        if at == 0:
                            sums[bump, block] = total
                        else:
                            sums[bump, block] += total

    for block in range(8):
        tile, part = block // 2, block % 2
        half, y_half = tile // 2, tile % 2
        owner = half * 2 + part
        for channel in range(3):
            mixed = None
            for bump in range(4):
                term = table(color_ref, tile, channel, bump) * sums[bump, block]
                mixed = term if mixed is None else mixed + term
            row = channel * 2 + y_half
            colours[owner, row : row + 1, :] = jnp.sum(mixed * share[block], axis=0, keepdims=True)
        colours[owner, 6 + y_half : 7 + y_half, :] = jnp.zeros((1, LANES), jnp.float32)

    colour_copies = [
        depth_copy(step, colours, colours_in, c_send, c_recv) for step in range(1, n_depth)
    ]
    for copy in colour_copies:
        copy.start()
    colours_in[depth] = colours[depth]

    for copy in clear_copies:
        copy.wait()
    own_half = depth // 2
    odd = lax.rem(sublane, 2) == 1
    back_rows = (
        jnp.where(odd, order_ref[own_half, 1], order_ref[own_half, 0]) == 1
    )
    ones = jnp.ones((SEGMENTS, LANES), jnp.float32)
    forth, aback = [ones], [ones]
    for at in range(n_depth):
        forth.append(forth[-1] * clear_in[at])
        aback.append(aback[-1] * clear_in[n_depth - 1 - at])
    for copy in colour_copies:
        copy.wait()
    image = None
    for at in range(n_depth):
        in_front = jnp.where(back_rows, aback[n_depth - 1 - at], forth[at])
        term = in_front * colours_in[at]
        image = term if image is None else image + term
    image = jnp.where(sublane >= 6, 1.0 - forth[n_depth], image)
    low = lax.broadcasted_iota(jnp.int32, (SEGMENTS, LANES), 1) < SIDE
    for channel in range(4):
        halves = []
        for y_half in range(2):
            row = channel * 2 + y_half
            line = jnp.broadcast_to(image[row : row + 1, :], (SEGMENTS, LANES))
            for bit in (4, 2, 1):
                line = jnp.where(
                    (sublane & bit) != 0, pltpu.roll(line, LANES - SIDE * bit, axis=1), line
                )
            halves.append(pltpu.roll(line, SIDE, axis=1) if y_half else line)
        out_ref[channel] = jnp.where(low, halves[0], halves[1])[:, : 2 * SIDE]

    for at in range(CHUNKS):
        x_copy(near_half, near_core, at).wait_send()

        @pl.when(has_far)
        def _(at=at):
            x_copy(far_half, far_core, at).wait_send()

        for side in range(2):

            @pl.when(has["sy", side])
            def _(side=side, at=at):
                for half in range(2):
                    y_copy(side, half, at).wait_send()


def per_device(
    counts, density, kernel_taps, tf_centre, tf_width, tf_color, tf_opacity, brick_tf, view_order
):
    rows_x, rows_y, rows_z = density.shape
    n_depth = counts[0]
    f32, bf16 = jnp.float32, jnp.bfloat16
    smem = pl.BlockSpec(memory_space=pltpu.SMEM)
    vmem = pl.BlockSpec(memory_space=pltpu.VMEM)
    picture = pl.pallas_call(
        functools.partial(kernel, counts),
        out_shape=jax.ShapeDtypeStruct((4, rows_x // n_depth, rows_y), f32),
        in_specs=[pl.BlockSpec(memory_space=pl.ANY), vmem] + [smem] * 6,
        out_specs=vmem,
        scratch_shapes=[
            pltpu.VMEM((rows_x, rows_y, rows_z), f32),
            pltpu.VMEM((8, rows_z, LANES), f32),
            pltpu.VMEM((2, rows_z, 2 * CELLS), bf16),
            pltpu.VMEM((2, rows_z, 2 * CELLS), bf16),
            pltpu.VMEM((2, 2, rows_z, CELLS), bf16),
            pltpu.VMEM((2, 2, rows_z, CELLS), bf16),
            pltpu.VMEM((4, 8, rows_z, LANES), f32),
            pltpu.VMEM((3 * CELLS, CELLS), bf16),
            pltpu.VMEM((3 * CELLS, CELLS), bf16),
            pltpu.VMEM((8, LANES), f32),
            pltpu.VMEM((8, SEGMENTS, LANES), f32),
            pltpu.VMEM((4, 8, SEGMENTS, LANES), f32),
            pltpu.VMEM((8, SEGMENTS, LANES), f32),
            pltpu.VMEM((n_depth, 8, LANES), f32),
            pltpu.VMEM((n_depth, 8, LANES), f32),
            pltpu.VMEM((n_depth, 8, LANES), f32),
            pltpu.VMEM((n_depth, 8, LANES), f32),
            pltpu.SemaphoreType.DMA((2,)),
            pltpu.SemaphoreType.DMA((2, CHUNKS)),
            pltpu.SemaphoreType.DMA((2, CHUNKS)),
            pltpu.SemaphoreType.DMA((2, 2, CHUNKS)),
            pltpu.SemaphoreType.DMA((2, 2, CHUNKS)),
            pltpu.SemaphoreType.DMA((n_depth - 1,)),
            pltpu.SemaphoreType.DMA((n_depth - 1,)),
            pltpu.SemaphoreType.DMA((n_depth - 1,)),
            pltpu.SemaphoreType.DMA((n_depth - 1,)),
        ],
        compiler_params=pltpu.CompilerParams(collective_id=0, has_side_effects=True),
    )(
        density,
        kernel_taps,
        tf_centre.T,
        tf_width.T,
        tf_color.transpose(2, 1, 0),
        tf_opacity.T,
        brick_tf,
        view_order,
    )
    return picture.reshape(4, 1, 1, rows_x // n_depth, rows_y)


def solution(mesh):
    counts = tuple(mesh.shape[axis] for axis in ("depth", "sx", "sy"))
    return jax.shard_map(
        functools.partial(per_device, counts),
        mesh=mesh,
        in_specs=(
            P("sx", "sy", "depth"),
            P(),
            P(),
            P(),
            P(),
            P(),
            P("sx", "sy", "depth"),
            P("sx", "sy"),
        ),
        out_specs=P(None, "sx", "depth", None, "sy"),
        check_vma=False,
    )
```

```python
import functools

import jax
import jax.numpy as jnp
from jax import lax
from jax.experimental import pallas as pl
from jax.experimental.pallas import tpu as pltpu
from jax.sharding import PartitionSpec as P

MESH = pl.DeviceIdType.MESH
LOG2E = 1.4426950408889634
CHUNKS = 4
SIDE = 16
CELLS = SIDE * SIDE
LANES = 128
SEGMENTS = 8


def band_tiles(taps_row, along_x, scale):
    shifted = pltpu.roll(
        jnp.broadcast_to(taps_row, (LANES, LANES)), 0, axis=1, stride=1, stride_axis=0
    ).astype(jnp.bfloat16)

    def part(index):
        return index // SIDE if along_x else index % SIDE

    def other(index):
        return index % SIDE if along_x else index // SIDE

    row = lax.broadcasted_iota(jnp.int32, (3 * CELLS, LANES), 0)
    tap = lax.broadcasted_iota(jnp.int32, (3 * CELLS, LANES), 1)
    left = (tap == part(row % CELLS) + SIDE * (row // CELLS)).astype(jnp.float32)
    first = lax.dot_general(
        left.astype(jnp.bfloat16),
        shifted,
        (((1,), (1,)), ((), ())),
        preferred_element_type=jnp.float32,
    ).astype(jnp.bfloat16)
    target = lax.broadcasted_iota(jnp.int32, (LANES, CELLS), 0)
    column = lax.broadcasted_iota(jnp.int32, (LANES, CELLS), 1)
    right = (target == part(column)).astype(jnp.float32).astype(jnp.bfloat16)
    full = jnp.dot(first, right, preferred_element_type=jnp.float32)
    row = lax.broadcasted_iota(jnp.int32, (3 * CELLS, CELLS), 0)
    column = lax.broadcasted_iota(jnp.int32, (3 * CELLS, CELLS), 1)
    keep = other(row % CELLS) == other(column)
    return jnp.where(keep, full * scale, 0.0).astype(jnp.bfloat16)


def kernel(
    counts,
    density_hbm,
    taps_hbm,
    centre_hbm,
    width_hbm,
    color_hbm,
    opacity_hbm,
    brick_hbm,
    order_hbm,
    out_ref,
    taps_ref,
    centre_ref,
    width_ref,
    color_ref,
    opacity_ref,
    brick_ref,
    order_ref,
    table_sem,
    density,
    turned,
    coarse,
    x_halo,
    across,
    y_halo,
    weighted,
    band_x,
    band_y,
    taps_wide,
    running,
    sums,
    share,
    colours,
    clear,
    colours_in,
    clear_in,
    load_sem,
    x_send,
    x_recv,
    y_send,
    y_recv,
    t_send,
    t_recv,
    c_send,
    c_recv,
):
    n_depth, n_sx, n_sy = counts
    depth, sx, sy = lax.axis_index("depth"), lax.axis_index("sx"), lax.axis_index("sy")
    rows_z = turned.shape[1]
    steps = rows_z // SEGMENTS
    chunk = rows_z // CHUNKS
    steps_chunk = steps // CHUNKS
    has = {
        ("sx", 0): sx > 0,
        ("sx", 1): sx < n_sx - 1,
        ("sy", 0): sy > 0,
        ("sy", 1): sy < n_sy - 1,
    }
    near = {
        ("sx", 0): {"sx": jnp.maximum(sx - 1, 0)},
        ("sx", 1): {"sx": jnp.minimum(sx + 1, n_sx - 1)},
        ("sy", 0): {"sy": jnp.maximum(sy - 1, 0)},
        ("sy", 1): {"sy": jnp.minimum(sy + 1, n_sy - 1)},
    }

    near_half = 1 - lax.rem(sx, 2)
    far_half = lax.rem(sx, 2)
    has_far = jnp.logical_and(sx > 0, sx < n_sx - 1)
    near_core = {"sx": sx + 2 * near_half - 1}
    far_core = {"sx": jnp.clip(sx + 2 * far_half - 1, 0, n_sx - 1)}

    loads = []
    for half in range(2):
        copy = pltpu.make_async_copy(
            density_hbm.at[pl.ds(half * SIDE, SIDE)],
            density.at[pl.ds(half * SIDE, SIDE)],
            load_sem.at[half],
        )
        copy.start()
        loads.append(copy)

    barrier = pltpu.get_barrier_semaphore()
    for key, there in has.items():

        @pl.when(there)
        def _(key=key):
            pl.semaphore_signal(barrier, inc=1, device_id=near[key], device_id_type=MESH)

    for step in range(1, n_depth):
        pl.semaphore_signal(
            barrier,
            inc=1,
            device_id={"depth": lax.rem(depth + step, n_depth)},
            device_id_type=MESH,
        )

    tables = (
        (taps_hbm, taps_ref),
        (centre_hbm, centre_ref),
        (width_hbm, width_ref),
        (color_hbm, color_ref),
        (opacity_hbm, opacity_ref),
        (brick_hbm, brick_ref),
        (order_hbm, order_ref),
    )
    table_loads = []
    for at, (source, target) in enumerate(tables):
        copy = pltpu.make_async_copy(source, target, table_sem.at[at])
        copy.start()
        table_loads.append(copy)

    for axis, halo in (("sx", x_halo), ("sy", y_halo)):
        for side in range(2):

            @pl.when(jnp.logical_not(has[axis, side]))
            def _(halo=halo, side=side):
                halo[side] = jnp.zeros(halo.shape[1:], halo.dtype)

    for half in range(2):
        loads[half].wait()
        for y_half in range(2):
            tile = half * 2 + y_half
            for part in range(2):
                x_at = half * SIDE + part * (SIDE // 2)
                piece = density[x_at : x_at + SIDE // 2, y_half * SIDE : (y_half + 1) * SIDE, :]
                turned[tile * 2 + part] = piece.reshape(LANES, rows_z).T

    waits = n_depth - 1
    for there in has.values():
        waits = waits + there.astype(jnp.int32)
    pl.semaphore_wait(barrier, waits)

    def x_copy(side, core, at):
        rows = pl.ds(at * chunk, chunk)
        return pltpu.make_async_remote_copy(
            src_ref=coarse.at[side, rows],
            dst_ref=x_halo.at[1 - side, rows],
            send_sem=x_send.at[side, at],
            recv_sem=x_recv.at[1 - side, at],
            device_id=core,
            device_id_type=MESH,
        )

    def x_arrival(side, core, at):
        rows = pl.ds(at * chunk, chunk)
        return pltpu.make_async_remote_copy(
            src_ref=x_halo.at[side, rows],
            dst_ref=x_halo.at[side, rows],
            send_sem=x_send.at[side, at],
            recv_sem=x_recv.at[side, at],
            device_id=core,
            device_id_type=MESH,
        )

    def y_copy(side, half, at):
        rows = pl.ds(at * chunk, chunk)
        return pltpu.make_async_remote_copy(
            src_ref=across.at[side, half, rows],
            dst_ref=y_halo.at[1 - side, half, rows],
            send_sem=y_send.at[side, half, at],
            recv_sem=y_recv.at[1 - side, half, at],
            device_id=near["sy", side],
            device_id_type=MESH,
        )

    def y_arrival(side, half, at):
        rows = pl.ds(at * chunk, chunk)
        return pltpu.make_async_remote_copy(
            src_ref=y_halo.at[side, half, rows],
            dst_ref=y_halo.at[side, half, rows],
            send_sem=y_send.at[side, half, at],
            recv_sem=y_recv.at[side, half, at],
            device_id=near["sy", side],
            device_id_type=MESH,
        )

    for at in range(CHUNKS):

        @pl.loop(at * (steps_chunk // 2), (at + 1) * (steps_chunk // 2))
        def _(pair):
            for block in range(8):
                tile, part = block // 2, block % 2
                half, y_half = tile // 2, tile % 2
                both = jnp.concatenate(
                    [
                        turned[block, pl.ds(pair * 2, SEGMENTS, stride=steps), :],
                        turned[block, pl.ds(pair * 2 + 1, SEGMENTS, stride=steps), :],
                    ],
                    axis=0,
                )
                lane = y_half * CELLS + part * LANES
                coarse[half, pl.ds(pl.multiple_of(pair * 16, 16), 16), lane : lane + LANES] = (
                    both.astype(jnp.bfloat16)
                )

        @pl.when(has_far)
        def _(at=at):
            x_copy(far_half, far_core, at).start()

        x_copy(near_half, near_core, at).start()

    for copy in table_loads:
        copy.wait()
    taps_wide[...] = jnp.zeros(taps_wide.shape, taps_wide.dtype)
    taps_wide[0:2, 0 : taps_ref.shape[1]] = taps_ref[...].astype(jnp.float32)
    band_x[...] = band_tiles(taps_wide[0:1, :], True, 1.0)
    band_y[...] = band_tiles(taps_wide[1:2, :], False, 0.5)

    first_brick = lax.broadcasted_iota(jnp.int32, (SEGMENTS, LANES), 0) < SEGMENTS // 2

    def table(ref, tile, *rest):
        half, y_half = tile // 2, lax.rem(tile, 2)
        return jnp.where(
            first_brick,
            ref[rest + (brick_ref[half, y_half, 0],)],
            ref[rest + (brick_ref[half, y_half, 1],)],
        )

    def reversed_tile(tile):
        return order_ref[tile // 2, lax.rem(tile, 2)] == 1

    def bumps_of(tile):
        sign = jnp.where(reversed_tile(tile), LOG2E, -LOG2E).astype(jnp.float32)
        centre = [table(centre_ref, tile, bump) for bump in range(4)]
        width = [table(width_ref, tile, bump) for bump in range(4)]
        narrow = [-LOG2E / (each * each) for each in width]
        thick = [table(opacity_ref, tile, bump) * sign for bump in range(4)]

        def body(step, carry):
            after = []
            for part in range(2):
                block = tile * 2 + part
                cells = turned[block, pl.ds(step, SEGMENTS, stride=steps), :]
                bumps = []
                optical = None
                for bump in range(4):
                    away = cells - centre[bump]
                    value = jnp.exp2(away * away * narrow[bump])
                    bumps.append(value)
                    term = thick[bump] * value
                    optical = term if optical is None else optical + term
                nearer = carry[part] * jnp.exp2(optical)
                weight = carry[part] - nearer
                rows = pl.ds(pl.multiple_of(step * SEGMENTS, SEGMENTS), SEGMENTS)
                for bump in range(4):
                    weighted[bump, block, rows, :] = weight * bumps[bump]
                after.append(nearer)
            return tuple(after)

        ones = jnp.ones((SEGMENTS, LANES), jnp.float32)
        ends = lax.fori_loop(0, steps, body, (ones, ones), unroll=4)
        for part in range(2):
            running[tile * 2 + part] = ends[part]

    def blur_x(half, at):
        rows = slice(at * chunk, (at + 1) * chunk)
        inner, outer = [], []
        for y_half in range(2):
            lanes = slice(y_half * CELLS, (y_half + 1) * CELLS)
            inner.append(
                jnp.concatenate([coarse[0, rows, lanes], coarse[1, rows, lanes]], axis=1)
            )
            outer.append(x_halo[half, rows, lanes])
        inner_at = pl.multiple_of((1 - half) * CELLS, CELLS)
        outer_at = pl.multiple_of(half * (2 * CELLS), CELLS)
        result = jnp.dot(
            jnp.concatenate(inner, axis=0),
            band_x[pl.ds(inner_at, 2 * CELLS), :],
            preferred_element_type=jnp.float32,
        ) + jnp.dot(
            jnp.concatenate(outer, axis=0),
            band_x[pl.ds(outer_at, CELLS), :],
            preferred_element_type=jnp.float32,
        )
        result = result.astype(jnp.bfloat16)
        for y_half in range(2):
            across[y_half, half, rows, :] = result[y_half * chunk : (y_half + 1) * chunk]
        for side in range(2):

            @pl.when(has["sy", side])
            def _(side=side):
                y_copy(side, half, at).start()

    for at in range(CHUNKS):
        x_arrival(near_half, near_core, at).wait_recv()
        blur_x(near_half, at)

    @pl.loop(near_half * 2, near_half * 2 + 2)
    def _(tile):
        bumps_of(tile)

    for at in range(CHUNKS):

        @pl.when(has_far)
        def _(at=at):
            x_arrival(far_half, far_core, at).wait_recv()

        blur_x(far_half, at)

    @pl.loop(far_half * 2, far_half * 2 + 2)
    def _(tile):
        bumps_of(tile)

    sublane = lax.broadcasted_iota(jnp.int32, (SEGMENTS, LANES), 0)
    for block in range(8):
        tile, part = block // 2, block % 2
        half, y_half = tile // 2, tile % 2
        back = order_ref[half, y_half] == 1
        end = running[block]
        through = jnp.where(back, 1.0 / end, end)
        forth, aback = through, through
        for shift in (1, 2, 4):
            forth = forth * jnp.where(sublane >= shift, pltpu.roll(forth, shift, axis=0), 1.0)
            aback = aback * jnp.where(
                sublane < SEGMENTS - shift, pltpu.roll(aback, SEGMENTS - shift, axis=0), 1.0
            )
        in_front = jnp.where(
            back,
            jnp.where(sublane < SEGMENTS - 1, pltpu.roll(aback, SEGMENTS - 1, axis=0), 1.0),
            jnp.where(sublane >= 1, pltpu.roll(forth, 1, axis=0), 1.0),
        )
        share[block] = in_front * jnp.where(back, -0.5 * through, 0.5)
        owner = half * 2 + part
        for channel in range(4):
            clear[owner, channel * 2 + y_half : channel * 2 + y_half + 1, :] = aback[0:1, :]

    def depth_copy(step, source, target, send, recv):
        peer = lax.rem(depth + step, n_depth)
        return pltpu.make_async_remote_copy(
            src_ref=source.at[peer],
            dst_ref=target.at[depth],
            send_sem=send.at[step - 1],
            recv_sem=recv.at[step - 1],
            device_id={"depth": peer},
            device_id_type=MESH,
        )

    clear_copies = [
        depth_copy(step, clear, clear_in, t_send, t_recv) for step in range(1, n_depth)
    ]
    for copy in clear_copies:
        copy.start()
    clear_in[depth] = clear[depth]

    for half in (near_half, far_half):
        for at in range(CHUNKS):
            for side in range(2):

                @pl.when(has["sy", side])
                def _(side=side, at=at, half=half):
                    y_arrival(side, half, at).wait_recv()

            rows = slice(at * chunk, (at + 1) * chunk)
            before, first, second, behind = (
                y_halo[0, half, rows, :],
                across[0, half, rows, :],
                across[1, half, rows, :],
                y_halo[1, half, rows, :],
            )
            occlusion = jnp.dot(
                jnp.concatenate(
                    [
                        jnp.concatenate([before, first, second], axis=1),
                        jnp.concatenate([first, second, behind], axis=1),
                    ],
                    axis=0,
                ),
                band_y[...],
                preferred_element_type=jnp.float32,
            )
            shade = 1.0 - jnp.tanh(occlusion)
            for y_half in range(2):
                for part in range(2):
                    block = half * 4 + y_half * 2 + part
                    for bump in range(4):
                        total = None
                        for step in range(steps_chunk):
                            row = step * SEGMENTS
                            term = (
                                weighted[
                                    bump,
                                    block,
                                    at * chunk + row : at * chunk + row + SEGMENTS,
                                    :,
                                ]
                                * shade[
                                    y_half * chunk + row : y_half * chunk + row + SEGMENTS,
                                    part * LANES : (part + 1) * LANES,
                                ]
                            )
                            total = term if total is None else total + term
                        if at == 0:
                            sums[bump, block] = total
                        else:
                            sums[bump, block] += total

    for block in range(8):
        tile, part = block // 2, block % 2
        half, y_half = tile // 2, tile % 2
        owner = half * 2 + part
        for channel in range(3):
            mixed = None
            for bump in range(4):
                term = table(color_ref, tile, channel, bump) * sums[bump, block]
                mixed = term if mixed is None else mixed + term
            row = channel * 2 + y_half
            colours[owner, row : row + 1, :] = jnp.sum(mixed * share[block], axis=0, keepdims=True)
        colours[owner, 6 + y_half : 7 + y_half, :] = jnp.zeros((1, LANES), jnp.float32)

    colour_copies = [
        depth_copy(step, colours, colours_in, c_send, c_recv) for step in range(1, n_depth)
    ]
    for copy in colour_copies:
        copy.start()
    colours_in[depth] = colours[depth]

    for copy in clear_copies:
        copy.wait()
    own_half = depth // 2
    odd = lax.rem(sublane, 2) == 1
    back_rows = (
        jnp.where(odd, order_ref[own_half, 1], order_ref[own_half, 0]) == 1
    )
    ones = jnp.ones((SEGMENTS, LANES), jnp.float32)
    forth, aback = [ones], [ones]
    for at in range(n_depth):
        forth.append(forth[-1] * clear_in[at])
        aback.append(aback[-1] * clear_in[n_depth - 1 - at])
    for copy in colour_copies:
        copy.wait()
    image = None
    for at in range(n_depth):
        in_front = jnp.where(back_rows, aback[n_depth - 1 - at], forth[at])
        term = in_front * colours_in[at]
        image = term if image is None else image + term
    image = jnp.where(sublane >= 6, 1.0 - forth[n_depth], image)
    low = lax.broadcasted_iota(jnp.int32, (SEGMENTS, LANES), 1) < SIDE
    for channel in range(4):
        halves = []
        for y_half in range(2):
            row = channel * 2 + y_half
            line = jnp.broadcast_to(image[row : row + 1, :], (SEGMENTS, LANES))
            for bit in (4, 2, 1):
                line = jnp.where(
                    (sublane & bit) != 0, pltpu.roll(line, LANES - SIDE * bit, axis=1), line
                )
            halves.append(pltpu.roll(line, SIDE, axis=1) if y_half else line)
        out_ref[channel] = jnp.where(low, halves[0], halves[1])[:, : 2 * SIDE]

    for at in range(CHUNKS):
        x_copy(near_half, near_core, at).wait_send()

        @pl.when(has_far)
        def _(at=at):
            x_copy(far_half, far_core, at).wait_send()

        for side in range(2):

            @pl.when(has["sy", side])
            def _(side=side, at=at):
                for half in range(2):
                    y_copy(side, half, at).wait_send()


def per_device(
    counts, density, kernel_taps, tf_centre, tf_width, tf_color, tf_opacity, brick_tf, view_order
):
    rows_x, rows_y, rows_z = density.shape
    n_depth = counts[0]
    f32, bf16 = jnp.float32, jnp.bfloat16
    vmem = pl.BlockSpec(memory_space=pltpu.VMEM)
    picture = pl.pallas_call(
        functools.partial(kernel, counts),
        out_shape=jax.ShapeDtypeStruct((4, rows_x // n_depth, rows_y), f32),
        in_specs=[pl.BlockSpec(memory_space=pl.ANY)] * 8,
        out_specs=vmem,
        scratch_shapes=[
            pltpu.VMEM(kernel_taps.shape, bf16),
            pltpu.SMEM(tf_centre.shape[::-1], f32),
            pltpu.SMEM(tf_width.shape[::-1], f32),
            pltpu.SMEM(tf_color.shape[::-1], f32),
            pltpu.SMEM(tf_opacity.shape[::-1], f32),
            pltpu.SMEM(brick_tf.shape, jnp.int32),
            pltpu.SMEM(view_order.shape, jnp.int32),
            pltpu.SemaphoreType.DMA((7,)),
            pltpu.VMEM((rows_x, rows_y, rows_z), f32),
            pltpu.VMEM((8, rows_z, LANES), f32),
            pltpu.VMEM((2, rows_z, 2 * CELLS), bf16),
            pltpu.VMEM((2, rows_z, 2 * CELLS), bf16),
            pltpu.VMEM((2, 2, rows_z, CELLS), bf16),
            pltpu.VMEM((2, 2, rows_z, CELLS), bf16),
            pltpu.VMEM((4, 8, rows_z, LANES), f32),
            pltpu.VMEM((3 * CELLS, CELLS), bf16),
            pltpu.VMEM((3 * CELLS, CELLS), bf16),
            pltpu.VMEM((8, LANES), f32),
            pltpu.VMEM((8, SEGMENTS, LANES), f32),
            pltpu.VMEM((4, 8, SEGMENTS, LANES), f32),
            pltpu.VMEM((8, SEGMENTS, LANES), f32),
            pltpu.VMEM((n_depth, 8, LANES), f32),
            pltpu.VMEM((n_depth, 8, LANES), f32),
            pltpu.VMEM((n_depth, 8, LANES), f32),
            pltpu.VMEM((n_depth, 8, LANES), f32),
            pltpu.SemaphoreType.DMA((2,)),
            pltpu.SemaphoreType.DMA((2, CHUNKS)),
            pltpu.SemaphoreType.DMA((2, CHUNKS)),
            pltpu.SemaphoreType.DMA((2, 2, CHUNKS)),
            pltpu.SemaphoreType.DMA((2, 2, CHUNKS)),
            pltpu.SemaphoreType.DMA((n_depth - 1,)),
            pltpu.SemaphoreType.DMA((n_depth - 1,)),
            pltpu.SemaphoreType.DMA((n_depth - 1,)),
            pltpu.SemaphoreType.DMA((n_depth - 1,)),
        ],
        compiler_params=pltpu.CompilerParams(collective_id=0, has_side_effects=True),
    )(
        density,
        kernel_taps,
        tf_centre.T,
        tf_width.T,
        tf_color.transpose(2, 1, 0),
        tf_opacity.T,
        brick_tf,
        view_order,
    )
    return picture.reshape(4, 1, 1, rows_x // n_depth, rows_y)


def solution(mesh):
    counts = tuple(mesh.shape[axis] for axis in ("depth", "sx", "sy"))
    return jax.shard_map(
        functools.partial(per_device, counts),
        mesh=mesh,
        in_specs=(
            P("sx", "sy", "depth"),
            P(),
            P(),
            P(),
            P(),
            P(),
            P("sx", "sy", "depth"),
            P("sx", "sy"),
        ),
        out_specs=P(None, "sx", "depth", None, "sy"),
        check_vma=False,
    )
```

```python
import functools

import jax
import jax.numpy as jnp
from jax import lax
from jax.experimental import pallas as pl
from jax.experimental.pallas import tpu as pltpu
from jax.sharding import PartitionSpec as P

MESH = pl.DeviceIdType.MESH
LOG2E = 1.4426950408889634
CHUNKS = 2
SIDE = 16
CELLS = SIDE * SIDE
LANES = 128
SEGMENTS = 8


def band_tiles(taps_row, along_x, scale):
    shifted = pltpu.roll(
        jnp.broadcast_to(taps_row, (LANES, LANES)), 0, axis=1, stride=1, stride_axis=0
    ).astype(jnp.bfloat16)

    def part(index):
        return index // SIDE if along_x else index % SIDE

    def other(index):
        return index % SIDE if along_x else index // SIDE

    row = lax.broadcasted_iota(jnp.int32, (3 * CELLS, LANES), 0)
    tap = lax.broadcasted_iota(jnp.int32, (3 * CELLS, LANES), 1)
    left = (tap == part(row % CELLS) + SIDE * (row // CELLS)).astype(jnp.float32)
    first = lax.dot_general(
        left.astype(jnp.bfloat16),
        shifted,
        (((1,), (1,)), ((), ())),
        preferred_element_type=jnp.float32,
    ).astype(jnp.bfloat16)
    target = lax.broadcasted_iota(jnp.int32, (LANES, CELLS), 0)
    column = lax.broadcasted_iota(jnp.int32, (LANES, CELLS), 1)
    right = (target == part(column)).astype(jnp.float32).astype(jnp.bfloat16)
    full = jnp.dot(first, right, preferred_element_type=jnp.float32)
    row = lax.broadcasted_iota(jnp.int32, (3 * CELLS, CELLS), 0)
    column = lax.broadcasted_iota(jnp.int32, (3 * CELLS, CELLS), 1)
    keep = other(row % CELLS) == other(column)
    return jnp.where(keep, full * scale, 0.0).astype(jnp.bfloat16)


def kernel(
    counts,
    density_hbm,
    taps_hbm,
    centre_hbm,
    width_hbm,
    color_hbm,
    opacity_hbm,
    brick_hbm,
    order_hbm,
    out_hbm,
    out_ref,
    taps_ref,
    centre_ref,
    width_ref,
    color_ref,
    opacity_ref,
    brick_ref,
    order_ref,
    table_sem,
    out_sem,
    density,
    turned,
    coarse,
    x_halo,
    across,
    y_halo,
    weighted,
    band_x,
    band_y,
    taps_wide,
    running,
    sums,
    share,
    colours,
    clear,
    colours_in,
    clear_in,
    load_sem,
    x_send,
    x_recv,
    y_send,
    y_recv,
    t_send,
    t_recv,
    c_send,
    c_recv,
):
    n_depth, n_sx, n_sy = counts
    depth, sx, sy = lax.axis_index("depth"), lax.axis_index("sx"), lax.axis_index("sy")
    rows_z = turned.shape[1]
    steps = rows_z // SEGMENTS
    chunk = rows_z // CHUNKS
    steps_chunk = steps // CHUNKS
    has = {
        ("sx", 0): sx > 0,
        ("sx", 1): sx < n_sx - 1,
        ("sy", 0): sy > 0,
        ("sy", 1): sy < n_sy - 1,
    }
    near = {
        ("sx", 0): {"sx": jnp.maximum(sx - 1, 0)},
        ("sx", 1): {"sx": jnp.minimum(sx + 1, n_sx - 1)},
        ("sy", 0): {"sy": jnp.maximum(sy - 1, 0)},
        ("sy", 1): {"sy": jnp.minimum(sy + 1, n_sy - 1)},
    }

    near_half = 1 - lax.rem(sx, 2)
    far_half = lax.rem(sx, 2)
    has_far = jnp.logical_and(sx > 0, sx < n_sx - 1)
    near_core = {"sx": sx + 2 * near_half - 1}
    far_core = {"sx": jnp.clip(sx + 2 * far_half - 1, 0, n_sx - 1)}

    barrier = pltpu.get_barrier_semaphore()
    for key, there in has.items():

        @pl.when(there)
        def _(key=key):
            pl.semaphore_signal(barrier, inc=1, device_id=near[key], device_id_type=MESH)

    for step in range(1, n_depth):
        pl.semaphore_signal(
            barrier,
            inc=1,
            device_id={"depth": lax.rem(depth + step, n_depth)},
            device_id_type=MESH,
        )

    loads = []
    for half in range(2):
        copy = pltpu.make_async_copy(
            density_hbm.at[pl.ds(half * SIDE, SIDE)],
            density.at[pl.ds(half * SIDE, SIDE)],
            load_sem.at[half],
        )
        copy.start()
        loads.append(copy)

    tables = (
        (taps_hbm, taps_ref),
        (centre_hbm, centre_ref),
        (width_hbm, width_ref),
        (color_hbm, color_ref),
        (opacity_hbm, opacity_ref),
        (brick_hbm, brick_ref),
        (order_hbm, order_ref),
    )
    table_loads = []
    for at, (source, target) in enumerate(tables):
        copy = pltpu.make_async_copy(source, target, table_sem.at[at])
        copy.start()
        table_loads.append(copy)

    for axis, halo in (("sx", x_halo), ("sy", y_halo)):
        for side in range(2):

            @pl.when(jnp.logical_not(has[axis, side]))
            def _(halo=halo, side=side):
                halo[side] = jnp.zeros(halo.shape[1:], halo.dtype)

    for half in range(2):
        loads[half].wait()
        for y_half in range(2):
            tile = half * 2 + y_half
            for part in range(2):
                x_at = half * SIDE + part * (SIDE // 2)
                piece = density[x_at : x_at + SIDE // 2, y_half * SIDE : (y_half + 1) * SIDE, :]
                turned[tile * 2 + part] = piece.reshape(LANES, rows_z).T

    waits = n_depth - 1
    for there in has.values():
        waits = waits + there.astype(jnp.int32)
    pl.semaphore_wait(barrier, waits)

    def x_copy(side, core, at):
        rows = pl.ds(at * chunk, chunk)
        return pltpu.make_async_remote_copy(
            src_ref=coarse.at[side, rows],
            dst_ref=x_halo.at[1 - side, rows],
            send_sem=x_send.at[side, at],
            recv_sem=x_recv.at[1 - side, at],
            device_id=core,
            device_id_type=MESH,
        )

    def x_arrival(side, core, at):
        rows = pl.ds(at * chunk, chunk)
        return pltpu.make_async_remote_copy(
            src_ref=x_halo.at[side, rows],
            dst_ref=x_halo.at[side, rows],
            send_sem=x_send.at[side, at],
            recv_sem=x_recv.at[side, at],
            device_id=core,
            device_id_type=MESH,
        )

    def y_copy(side, half, at):
        rows = pl.ds(at * chunk, chunk)
        return pltpu.make_async_remote_copy(
            src_ref=across.at[side, half, rows],
            dst_ref=y_halo.at[1 - side, half, rows],
            send_sem=y_send.at[side, half, at],
            recv_sem=y_recv.at[1 - side, half, at],
            device_id=near["sy", side],
            device_id_type=MESH,
        )

    def y_arrival(side, half, at):
        rows = pl.ds(at * chunk, chunk)
        return pltpu.make_async_remote_copy(
            src_ref=y_halo.at[side, half, rows],
            dst_ref=y_halo.at[side, half, rows],
            send_sem=y_send.at[side, half, at],
            recv_sem=y_recv.at[side, half, at],
            device_id=near["sy", side],
            device_id_type=MESH,
        )

    for at in range(CHUNKS):

        @pl.loop(at * (steps_chunk // 2), (at + 1) * (steps_chunk // 2))
        def _(pair):
            for block in range(8):
                tile, part = block // 2, block % 2
                half, y_half = tile // 2, tile % 2
                both = jnp.concatenate(
                    [
                        turned[block, pl.ds(pair * 2, SEGMENTS, stride=steps), :],
                        turned[block, pl.ds(pair * 2 + 1, SEGMENTS, stride=steps), :],
                    ],
                    axis=0,
                )
                lane = y_half * CELLS + part * LANES
                coarse[half, pl.ds(pl.multiple_of(pair * 16, 16), 16), lane : lane + LANES] = (
                    both.astype(jnp.bfloat16)
                )

        @pl.when(has_far)
        def _(at=at):
            x_copy(far_half, far_core, at).start()

        x_copy(near_half, near_core, at).start()

    for copy in table_loads:
        copy.wait()
    taps_wide[...] = jnp.zeros(taps_wide.shape, taps_wide.dtype)
    taps_wide[0:2, 0 : taps_ref.shape[1]] = taps_ref[...].astype(jnp.float32)
    band_x[...] = band_tiles(taps_wide[0:1, :], True, 1.0)
    band_y[...] = band_tiles(taps_wide[1:2, :], False, 0.5)

    first_brick = lax.broadcasted_iota(jnp.int32, (SEGMENTS, LANES), 0) < SEGMENTS // 2

    def table(ref, tile, *rest):
        half, y_half = tile // 2, lax.rem(tile, 2)
        return jnp.where(
            first_brick,
            ref[rest + (brick_ref[half, y_half, 0],)],
            ref[rest + (brick_ref[half, y_half, 1],)],
        )

    def reversed_tile(tile):
        return order_ref[tile // 2, lax.rem(tile, 2)] == 1

    def bumps_of(tile):
        sign = jnp.where(reversed_tile(tile), LOG2E, -LOG2E).astype(jnp.float32)
        centre = [table(centre_ref, tile, bump) for bump in range(4)]
        width = [table(width_ref, tile, bump) for bump in range(4)]
        narrow = [-LOG2E / (each * each) for each in width]
        thick = [table(opacity_ref, tile, bump) * sign for bump in range(4)]

        def body(step, carry):
            after = []
            for part in range(2):
                block = tile * 2 + part
                cells = turned[block, pl.ds(step, SEGMENTS, stride=steps), :]
                bumps = []
                optical = None
                for bump in range(4):
                    away = cells - centre[bump]
                    value = jnp.exp2(away * away * narrow[bump])
                    bumps.append(value)
                    term = thick[bump] * value
                    optical = term if optical is None else optical + term
                nearer = carry[part] * jnp.exp2(optical)
                weight = carry[part] - nearer
                rows = pl.ds(pl.multiple_of(step * SEGMENTS, SEGMENTS), SEGMENTS)
                for bump in range(4):
                    weighted[bump, block, rows, :] = weight * bumps[bump]
                after.append(nearer)
            return tuple(after)

        ones = jnp.ones((SEGMENTS, LANES), jnp.float32)
        ends = lax.fori_loop(0, steps, body, (ones, ones), unroll=4)
        for part in range(2):
            running[tile * 2 + part] = ends[part]

    def blur_x(half, at):
        rows = slice(at * chunk, (at + 1) * chunk)
        inner, outer = [], []
        for y_half in range(2):
            lanes = slice(y_half * CELLS, (y_half + 1) * CELLS)
            inner.append(
                jnp.concatenate([coarse[0, rows, lanes], coarse[1, rows, lanes]], axis=1)
            )
            outer.append(x_halo[half, rows, lanes])
        inner_at = pl.multiple_of((1 - half) * CELLS, CELLS)
        outer_at = pl.multiple_of(half * (2 * CELLS), CELLS)
        result = jnp.dot(
            jnp.concatenate(inner, axis=0),
            band_x[pl.ds(inner_at, 2 * CELLS), :],
            preferred_element_type=jnp.float32,
        ) + jnp.dot(
            jnp.concatenate(outer, axis=0),
            band_x[pl.ds(outer_at, CELLS), :],
            preferred_element_type=jnp.float32,
        )
        result = result.astype(jnp.bfloat16)
        for y_half in range(2):
            across[y_half, half, rows, :] = result[y_half * chunk : (y_half + 1) * chunk]
        for side in range(2):

            @pl.when(has["sy", side])
            def _(side=side):
                y_copy(side, half, at).start()

    for at in range(CHUNKS):
        x_arrival(near_half, near_core, at).wait_recv()
        blur_x(near_half, at)

    @pl.loop(near_half * 2, near_half * 2 + 2)
    def _(tile):
        bumps_of(tile)

    for at in range(CHUNKS):

        @pl.when(has_far)
        def _(at=at):
            x_arrival(far_half, far_core, at).wait_recv()

        blur_x(far_half, at)

    @pl.loop(far_half * 2, far_half * 2 + 2)
    def _(tile):
        bumps_of(tile)

    sublane = lax.broadcasted_iota(jnp.int32, (SEGMENTS, LANES), 0)
    for block in range(8):
        tile, part = block // 2, block % 2
        half, y_half = tile // 2, tile % 2
        back = order_ref[half, y_half] == 1
        end = running[block]
        through = jnp.where(back, 1.0 / end, end)
        forth, aback = through, through
        for shift in (1, 2, 4):
            forth = forth * jnp.where(sublane >= shift, pltpu.roll(forth, shift, axis=0), 1.0)
            aback = aback * jnp.where(
                sublane < SEGMENTS - shift, pltpu.roll(aback, SEGMENTS - shift, axis=0), 1.0
            )
        in_front = jnp.where(
            back,
            jnp.where(sublane < SEGMENTS - 1, pltpu.roll(aback, SEGMENTS - 1, axis=0), 1.0),
            jnp.where(sublane >= 1, pltpu.roll(forth, 1, axis=0), 1.0),
        )
        share[block] = in_front * jnp.where(back, -0.5 * through, 0.5)
        owner = half * 2 + part
        for channel in range(4):
            clear[owner, channel * 2 + y_half : channel * 2 + y_half + 1, :] = aback[0:1, :]

    def depth_copy(step, source, target, send, recv):
        peer = lax.rem(depth + step, n_depth)
        return pltpu.make_async_remote_copy(
            src_ref=source.at[peer],
            dst_ref=target.at[depth],
            send_sem=send.at[step - 1],
            recv_sem=recv.at[step - 1],
            device_id={"depth": peer},
            device_id_type=MESH,
        )

    clear_copies = [
        depth_copy(step, clear, clear_in, t_send, t_recv) for step in range(1, n_depth)
    ]
    for copy in clear_copies:
        copy.start()
    clear_in[depth] = clear[depth]

    for half in (near_half, far_half):
        for at in range(CHUNKS):
            for side in range(2):

                @pl.when(has["sy", side])
                def _(side=side, at=at, half=half):
                    y_arrival(side, half, at).wait_recv()

            rows = slice(at * chunk, (at + 1) * chunk)
            before, first, second, behind = (
                y_halo[0, half, rows, :],
                across[0, half, rows, :],
                across[1, half, rows, :],
                y_halo[1, half, rows, :],
            )
            occlusion = jnp.dot(
                jnp.concatenate(
                    [
                        jnp.concatenate([before, first, second], axis=1),
                        jnp.concatenate([first, second, behind], axis=1),
                    ],
                    axis=0,
                ),
                band_y[...],
                preferred_element_type=jnp.float32,
            )
            shade = 1.0 - jnp.tanh(occlusion)
            for y_half in range(2):
                for part in range(2):
                    block = half * 4 + y_half * 2 + part
                    for bump in range(4):
                        total = None
                        for step in range(steps_chunk):
                            row = step * SEGMENTS
                            term = (
                                weighted[
                                    bump,
                                    block,
                                    at * chunk + row : at * chunk + row + SEGMENTS,
                                    :,
                                ]
                                * shade[
                                    y_half * chunk + row : y_half * chunk + row + SEGMENTS,
                                    part * LANES : (part + 1) * LANES,
                                ]
                            )
                            total = term if total is None else total + term
                        if at == 0:
                            sums[bump, block] = total
                        else:
                            sums[bump, block] += total

    for block in range(8):
        tile, part = block // 2, block % 2
        half, y_half = tile // 2, tile % 2
        owner = half * 2 + part
        for channel in range(3):
            mixed = None
            for bump in range(4):
                term = table(color_ref, tile, channel, bump) * sums[bump, block]
                mixed = term if mixed is None else mixed + term
            row = channel * 2 + y_half
            colours[owner, row : row + 1, :] = jnp.sum(mixed * share[block], axis=0, keepdims=True)
        colours[owner, 6 + y_half : 7 + y_half, :] = jnp.zeros((1, LANES), jnp.float32)

    colour_copies = [
        depth_copy(step, colours, colours_in, c_send, c_recv) for step in range(1, n_depth)
    ]
    for copy in colour_copies:
        copy.start()
    colours_in[depth] = colours[depth]

    for copy in clear_copies:
        copy.wait()
    own_half = depth // 2
    odd = lax.rem(sublane, 2) == 1
    back_rows = (
        jnp.where(odd, order_ref[own_half, 1], order_ref[own_half, 0]) == 1
    )
    ones = jnp.ones((SEGMENTS, LANES), jnp.float32)
    forth, aback = [ones], [ones]
    for at in range(n_depth):
        forth.append(forth[-1] * clear_in[at])
        aback.append(aback[-1] * clear_in[n_depth - 1 - at])
    for copy in colour_copies:
        copy.wait()
    image = None
    for at in range(n_depth):
        in_front = jnp.where(back_rows, aback[n_depth - 1 - at], forth[at])
        term = in_front * colours_in[at]
        image = term if image is None else image + term
    image = jnp.where(sublane >= 6, 1.0 - forth[n_depth], image)
    low = lax.broadcasted_iota(jnp.int32, (SEGMENTS, LANES), 1) < SIDE
    for channel in range(4):
        halves = []
        for y_half in range(2):
            row = channel * 2 + y_half
            line = jnp.broadcast_to(image[row : row + 1, :], (SEGMENTS, LANES))
            for bit in (4, 2, 1):
                line = jnp.where(
                    (sublane & bit) != 0, pltpu.roll(line, LANES - SIDE * bit, axis=1), line
                )
            halves.append(pltpu.roll(line, SIDE, axis=1) if y_half else line)
        out_ref[channel] = jnp.where(low, halves[0], halves[1])[:, : 2 * SIDE]

    result_copy = pltpu.make_async_copy(out_ref, out_hbm, out_sem)
    result_copy.start()
    for at in range(CHUNKS):
        x_copy(near_half, near_core, at).wait_send()

        @pl.when(has_far)
        def _(at=at):
            x_copy(far_half, far_core, at).wait_send()

        for side in range(2):

            @pl.when(has["sy", side])
            def _(side=side, at=at):
                for half in range(2):
                    y_copy(side, half, at).wait_send()

    result_copy.wait()


def per_device(
    counts, density, kernel_taps, tf_centre, tf_width, tf_color, tf_opacity, brick_tf, view_order
):
    rows_x, rows_y, rows_z = density.shape
    n_depth = counts[0]
    f32, bf16 = jnp.float32, jnp.bfloat16
    picture = pl.pallas_call(
        functools.partial(kernel, counts),
        out_shape=jax.ShapeDtypeStruct((4, rows_x // n_depth, rows_y), f32),
        in_specs=[pl.BlockSpec(memory_space=pl.ANY)] * 8,
        out_specs=pl.BlockSpec(memory_space=pl.ANY),
        scratch_shapes=[
            pltpu.VMEM((4, rows_x // n_depth, rows_y), f32),
            pltpu.VMEM(kernel_taps.shape, bf16),
            pltpu.SMEM(tf_centre.shape[::-1], f32),
            pltpu.SMEM(tf_width.shape[::-1], f32),
            pltpu.SMEM(tf_color.shape[::-1], f32),
            pltpu.SMEM(tf_opacity.shape[::-1], f32),
            pltpu.SMEM(brick_tf.shape, jnp.int32),
            pltpu.SMEM(view_order.shape, jnp.int32),
            pltpu.SemaphoreType.DMA((7,)),
            pltpu.SemaphoreType.DMA,
            pltpu.VMEM((rows_x, rows_y, rows_z), f32),
            pltpu.VMEM((8, rows_z, LANES), f32),
            pltpu.VMEM((2, rows_z, 2 * CELLS), bf16),
            pltpu.VMEM((2, rows_z, 2 * CELLS), bf16),
            pltpu.VMEM((2, 2, rows_z, CELLS), bf16),
            pltpu.VMEM((2, 2, rows_z, CELLS), bf16),
            pltpu.VMEM((4, 8, rows_z, LANES), f32),
            pltpu.VMEM((3 * CELLS, CELLS), bf16),
            pltpu.VMEM((3 * CELLS, CELLS), bf16),
            pltpu.VMEM((8, LANES), f32),
            pltpu.VMEM((8, SEGMENTS, LANES), f32),
            pltpu.VMEM((4, 8, SEGMENTS, LANES), f32),
            pltpu.VMEM((8, SEGMENTS, LANES), f32),
            pltpu.VMEM((n_depth, 8, LANES), f32),
            pltpu.VMEM((n_depth, 8, LANES), f32),
            pltpu.VMEM((n_depth, 8, LANES), f32),
            pltpu.VMEM((n_depth, 8, LANES), f32),
            pltpu.SemaphoreType.DMA((2,)),
            pltpu.SemaphoreType.DMA((2, CHUNKS)),
            pltpu.SemaphoreType.DMA((2, CHUNKS)),
            pltpu.SemaphoreType.DMA((2, 2, CHUNKS)),
            pltpu.SemaphoreType.DMA((2, 2, CHUNKS)),
            pltpu.SemaphoreType.DMA((n_depth - 1,)),
            pltpu.SemaphoreType.DMA((n_depth - 1,)),
            pltpu.SemaphoreType.DMA((n_depth - 1,)),
            pltpu.SemaphoreType.DMA((n_depth - 1,)),
        ],
        compiler_params=pltpu.CompilerParams(collective_id=0, has_side_effects=True),
    )(
        density,
        kernel_taps,
        tf_centre.T,
        tf_width.T,
        tf_color.transpose(2, 1, 0),
        tf_opacity.T,
        brick_tf,
        view_order,
    )
    return picture.reshape(4, 1, 1, rows_x // n_depth, rows_y)


def solution(mesh):
    counts = tuple(mesh.shape[axis] for axis in ("depth", "sx", "sy"))
    return jax.shard_map(
        functools.partial(per_device, counts),
        mesh=mesh,
        in_specs=(
            P("sx", "sy", "depth"),
            P(),
            P(),
            P(),
            P(),
            P(),
            P("sx", "sy", "depth"),
            P("sx", "sy"),
        ),
        out_specs=P(None, "sx", "depth", None, "sy"),
        check_vma=False,
    )
```
